128 devices in a mesh: row: 4 (over z), col: 8 (over y, core), seq: 4 (over x).
Axes of the slice: x: 4, y: 4, z: 4, core: 2. Of those that a mesh axis runs over, the one named last changes fastest.
Arguments:
- motion_ids: int32 [1536], P('col'), may hold values from 0 to 511
- audio_ids: int32 [1536], P('col'), may hold values from 0 to 1023
- segment_ids: int32 [1536], replicated, may hold values from 0 to 3, never falling along the last dimension, each value on 1 to 768 neighbouring positions
- motion_table: bfloat16 [512, 8192], P(None, ('row', 'seq')), may hold values from -40 to 40
- audio_table: bfloat16 [1024, 8192], P(None, ('row', 'seq')), may hold values from -40 to 40
- norm_gain: float32 [8192], P(('row', 'seq')), may hold values from 0.5 to 1.5
- w_query: bfloat16 [8192, 8192], P(('row', 'seq'), 'col'), may hold values from -0.1875 to 0.1875
- w_key: bfloat16 [8192, 1024], P(('row', 'seq'), 'col'), may hold values from -0.0625 to 0.0625
- w_value: bfloat16 [8192, 1024], P(('row', 'seq'), 'col'), may hold values from -0.0625 to 0.0625
- w_out: bfloat16 [8192, 8192], P('col', ('row', 'seq')), may hold values from -0.0625 to 0.0625
- out_grad: bfloat16 [1536, 8192], P('col', ('row', 'seq')), may hold values from -6 to 6
Outputs:
- layer_out: bfloat16 [1536, 8192], P('col', ('row', 'seq'))
- grad_input: bfloat16 [1536, 8192], P('col', ('row', 'seq'))
- grad_gain: float32 [8192], P(('row', 'seq'))
- grad_wq: float32 [8192, 8192], P(('row', 'seq'), 'col')
- grad_wk: float32 [8192, 1024], P(('row', 'seq'), 'col')
- grad_wv: float32 [8192, 1024], P(('row', 'seq'), 'col')
- grad_wo: float32 [8192, 8192], P('col', ('row', 'seq'))
The draws below stay inside these ranges and needn't reach their ends.
Inputs may be any that keep to these rules, and one draw needn't show every extreme that they name: `segment_ids`: document ids never fall along the sequence; no document is longer than 768 positions, and one is exactly that long.
All inputs are finite; a program needn't handle non-finite values.
Results may differ from the reference program's by a relative error of at most 0.023.
Values may be sent and summed in bfloat16 or wider, within the bound.
No kernel may reach another device: no remote copies, remote signals or barrier semaphores. Data moves between devices by JAX's collectives and lax.ppermute only.
A program may use at most 128 MiB of HBM per device.

```python
import math
from functools import partial
import jax
import jax.numpy as jnp
import numpy as np
from jax import lax

D = 8192
H = 64
KV = 8
HD = 128
VM = 512
VA = 1024
L = 1536
KVD = 1024


def table_values(key, row_total, col_total):
    key_base, key_cols, key_rows = jax.random.split(key, 3)
    col_place = jnp.arange(col_total, dtype=jnp.float32) / (col_total - 1)
    values = jnp.clip(jax.random.normal(key_base, (row_total, col_total), jnp.float32), -4.0, 4.0)
    ramp_scale = jnp.exp(jnp.log(3.0) * col_place) / 1.7
    col_scale = ramp_scale * jnp.exp(jax.random.uniform(key_cols, (col_total,), jnp.float32, 0.0, jnp.log(3.3))) / 1.8
    row_scale = jnp.exp(jax.random.uniform(key_rows, (row_total, 1), jnp.float32, jnp.log(0.3), jnp.log(3.0)))
    return (values * col_scale[None, :] * row_scale).astype(jnp.bfloat16)


def draw_motion_table(key, part):
    return table_values(jax.random.fold_in(key, 11), VM, D)


def draw_audio_table(key, part):
    return table_values(jax.random.fold_in(key, 23), VA, D)


def plant(values, key, least, top_value):
    longest = values.shape.index(max(values.shape))
    spots = []
    for shift in (0, 1):
        where = [jax.random.randint(jax.random.fold_in(key, axis), (), 0, length) for axis, length in enumerate(values.shape)]
        where[longest] = (where[longest] + shift) % values.shape[longest]
        spots.append(tuple(where))
    return values.at[spots[0]].set(least).at[spots[1]].set(top_value)


def block_scale(key, extent, cuts, smallest, largest):
    factor_of, own = 1.0, jax.random.fold_in(key, 6)
    for axis_at, blocks in cuts:
        draws = jnp.exp(jax.random.uniform(jax.random.fold_in(own, axis_at), (blocks,), jnp.float32, smallest / len(cuts), largest / len(cuts)))
        factor_of = factor_of * jnp.repeat(draws, extent[axis_at] // blocks).reshape([-1 if axis == axis_at else 1 for axis in range(len(extent))])
    return factor_of


def rank_bounds(number_of, slope):
    loads = [(1 << 20) // math.isqrt(grade ** slope) + 1 for grade in range(1, number_of + 1)]
    spread = 1 + sum(loads) // (1 << 30)
    return np.cumsum(np.array([max(1, weight // spread) for weight in loads]))


def ranked(stream_key, dims, number_of, skew):
    listing = rank_bounds(number_of, skew)
    pick = jax.random.randint(jax.random.fold_in(stream_key, 1), dims, 0, int(listing[number_of - 1]))
    standing = jnp.searchsorted(jnp.asarray(listing, jnp.int32), pick, side="right")
    return jax.random.permutation(jax.random.fold_in(stream_key, 2), number_of)[standing].astype(jnp.int32)


def split_up(count, total, limit, lean):
    loads = [(1 << 20) // math.isqrt(standing ** lean) + 1 for standing in range(2, count + 1)]
    rest, given = total - limit - (count - 1), [1] * (count - 1)
    while rest > 0:
        free = [i for i in range(count - 1) if given[i] < limit]
        whole, left = sum([loads[i] for i in free]), rest
        for i in free:
            extra = min(limit - given[i], max(1, left * loads[i] // whole), rest)
            given[i] = given[i] + extra
            rest = rest - extra
    return np.array([limit] + given)


def uneven_parts(own_key, count, total, reach, skew):
    if count == 2:
        one = jax.random.randint(own_key, (), max(1, total - reach), min(reach, total - 1) + 1)
        return jnp.stack([one, total - one])
    sizes = jnp.asarray(split_up(count, total, reach, skew), jnp.int32)
    pairs = (count - 1) // 2
    source_of, sink = sizes[1:1 + 2 * pairs:2], sizes[2:2 + 2 * pairs:2]
    room = jnp.minimum(source_of - 1, reach - sink)
    moved = jax.random.randint(jax.random.fold_in(own_key, 1), (pairs,), 0, 1 << 20) % (room + 1)
    sizes = sizes.at[1:1 + 2 * pairs:2].set(source_of - moved).at[2:2 + 2 * pairs:2].set(sink + moved)
    return sizes[jax.random.permutation(jax.random.fold_in(own_key, 2), count)]


def gaussian(own_key, dims, deviation, most, cuts=(), kind=jnp.bfloat16):
    entries = deviation * jax.random.normal(own_key, dims, jnp.float32)
    if cuts:
        entries = entries * block_scale(own_key, dims, cuts, -0.22, 0.18)
    return jnp.clip(entries, -most, most).astype(kind)


def setup_inputs(seed: int = 0) -> dict:
    key_list = jax.random.split(jax.random.key(seed), 12)
    motion_ids = plant(ranked(key_list[0], (L,), VM, 2), jax.random.fold_in(key_list[0], 3), 0, VM - 1).astype(jnp.int32)
    audio_ids = plant(ranked(key_list[1], (L,), VA, 2), jax.random.fold_in(key_list[1], 3), 0, VA - 1).astype(jnp.int32)
    segment_ids = jnp.searchsorted(jnp.cumsum(uneven_parts(key_list[2], 4, L, L // 2, 0)), jnp.arange(L), side="right").astype(jnp.int32)
    motion_table = draw_motion_table(jax.random.fold_in(key_list[11], 71), 0)
    audio_table = draw_audio_table(jax.random.fold_in(key_list[11], 71), 0)
    norm_gain = jnp.clip(1.0 + 0.1 * jax.random.normal(key_list[5], (D,), jnp.float32), 0.5, 1.5)
    w_query = gaussian(key_list[6], (D, D), (D // 9) ** -0.5, 0.1875, ((0, 16), (1, 8)))
    w_key = gaussian(key_list[7], (D, KVD), D ** -0.5, 0.0625, ((0, 16), (1, 8)))
    w_value = gaussian(key_list[8], (D, KVD), D ** -0.5, 0.0625, ((0, 16), (1, 8)))
    w_out = gaussian(key_list[9], (D, D), D ** -0.5, 0.0625, ((0, 8), (1, 16)))
    out_grad = gaussian(key_list[10], (L, D), 1.0, 6.0, ((0, 8), (1, 16)))
    return dict(motion_ids=motion_ids, audio_ids=audio_ids, segment_ids=segment_ids, motion_table=motion_table, audio_table=audio_table, norm_gain=norm_gain, w_query=w_query, w_key=w_key, w_value=w_value, w_out=w_out, out_grad=out_grad)


epsilon = 1e-05
softcap = 20.0
rope_base = 500000.0

def rotary_tables(positions, head_size):
    half_size = head_size // 2
    frequency = rope_base ** (-(jnp.arange(half_size, dtype=jnp.float32) * 2.0) / head_size)
    angles = positions.astype(jnp.float32)[:, None] * frequency[None, :]
    return (jnp.cos(angles), jnp.sin(angles))

def rotate_pairs(values, cosines, sines):
    half_size = values.shape[-1] // 2
    first_half = values[..., :half_size]
    second_half = values[..., half_size:]
    cos_part = cosines[:, None, :]
    sin_part = sines[:, None, :]
    return jnp.concatenate([first_half * cos_part - second_half * sin_part, second_half * cos_part + first_half * sin_part], axis=-1)

def rotate_back(values, cosines, sines):
    half_size = values.shape[-1] // 2
    first_half = values[..., :half_size]
    second_half = values[..., half_size:]
    cos_part = cosines[:, None, :]
    sin_part = sines[:, None, :]
    return jnp.concatenate([first_half * cos_part + second_half * sin_part, second_half * cos_part - first_half * sin_part], axis=-1)

def group_pass(allowed, operands):
    query_grp, key_grp, value_grp, dout_grp = operands
    query_full = query_grp.astype(jnp.float32)
    key_full = key_grp.astype(jnp.float32)
    value_full = value_grp.astype(jnp.float32)
    dout_full = dout_grp.astype(jnp.float32)
    score_scale = HD ** (-0.5)
    raw_scores = jnp.einsum('qhd,kd->hqk', query_full, key_full) * score_scale
    capped = softcap * jnp.tanh(raw_scores / softcap)
    weights = jnp.where(allowed[None], jnp.exp(capped), 0.0)
    totals = lax.optimization_barrier(jnp.sum(weights, axis=2))
    weights_round = lax.optimization_barrier(weights.astype(jnp.bfloat16)).astype(jnp.float32)
    attended = jnp.einsum('hqk,kd->qhd', weights_round, value_full)
    attn_out = (attended / totals.T[:, :, None]).astype(jnp.bfloat16)
    attn_probs = weights / totals[:, :, None]
    prob_grads = jnp.einsum('qhd,kd->hqk', dout_full, value_full)
    row_dots = lax.optimization_barrier(jnp.sum(attn_probs * prob_grads, axis=2, keepdims=True))
    grad_scores = (attn_probs * (prob_grads - row_dots) * (1.0 - (capped / softcap) ** 2) * score_scale).astype(jnp.bfloat16)
    grad_scores = lax.optimization_barrier(grad_scores).astype(jnp.float32)
    probs_round = lax.optimization_barrier(attn_probs.astype(jnp.bfloat16)).astype(jnp.float32)
    grad_query = jnp.einsum('hqk,kd->qhd', grad_scores, key_full)
    grad_key = jnp.einsum('hqk,qhd->kd', grad_scores, query_full)
    grad_value = jnp.einsum('hqk,qhd->kd', probs_round, dout_full)
    return (attn_out, grad_query, grad_key, grad_value)

def reference(motion_ids, audio_ids, segment_ids, motion_table, audio_table, norm_gain, w_query, w_key, w_value, w_out, out_grad):
    seq_len = segment_ids.shape[0]
    group_size = H // KV
    embedded = (jnp.take(motion_table, motion_ids, axis=0).astype(jnp.float32) + jnp.take(audio_table, audio_ids, axis=0).astype(jnp.float32)).astype(jnp.bfloat16)
    residual = embedded.astype(jnp.float32)
    inverse = lax.rsqrt(lax.optimization_barrier(jnp.sum(residual * residual, axis=1)) / D + epsilon)
    normed = (residual * inverse[:, None] * norm_gain[None, :]).astype(jnp.bfloat16)
    positions = jnp.arange(seq_len, dtype=jnp.int32)
    cosines, sines = rotary_tables(positions, HD)
    queries = rotate_pairs(jnp.dot(normed, w_query, preferred_element_type=jnp.float32).reshape(seq_len, H, HD), cosines, sines).astype(jnp.bfloat16)
    key_heads = rotate_pairs(jnp.dot(normed, w_key, preferred_element_type=jnp.float32).reshape(seq_len, KV, HD), cosines, sines).astype(jnp.bfloat16)
    value_heads = jnp.dot(normed, w_value, preferred_element_type=jnp.float32).reshape(seq_len, KV, HD).astype(jnp.bfloat16)
    out_heads = jnp.dot(out_grad, w_out.T, preferred_element_type=jnp.float32).astype(jnp.bfloat16).reshape(seq_len, KV, group_size, HD)
    allowed = (positions[None, :] <= positions[:, None]) & (segment_ids[None, :] == segment_ids[:, None])
    stacked = (queries.reshape(seq_len, KV, group_size, HD).transpose(1, 0, 2, 3), key_heads.transpose(1, 0, 2), value_heads.transpose(1, 0, 2), out_heads.transpose(1, 0, 2, 3))
    attn_out, grad_query, grad_key, grad_value = lax.map(partial(group_pass, allowed), stacked)
    attended = attn_out.transpose(1, 0, 2, 3).reshape(seq_len, D)
    grad_query = rotate_back(grad_query.transpose(1, 0, 2, 3).reshape(seq_len, H, HD), cosines, sines).reshape(seq_len, D).astype(jnp.bfloat16)
    grad_key = rotate_back(grad_key.transpose(1, 0, 2), cosines, sines).reshape(seq_len, KV * HD).astype(jnp.bfloat16)
    grad_value = grad_value.transpose(1, 0, 2).reshape(seq_len, KV * HD).astype(jnp.bfloat16)
    layer_out = (residual + jnp.dot(attended, w_out, preferred_element_type=jnp.float32)).astype(jnp.bfloat16)
    grad_wo = jnp.dot(attended.T, out_grad, preferred_element_type=jnp.float32)
    grad_wq = jnp.dot(normed.T, grad_query, preferred_element_type=jnp.float32)
    grad_wk = jnp.dot(normed.T, grad_key, preferred_element_type=jnp.float32)
    grad_wv = jnp.dot(normed.T, grad_value, preferred_element_type=jnp.float32)
    grad_normed = jnp.dot(grad_query, w_query.T, preferred_element_type=jnp.float32) + jnp.dot(grad_key, w_key.T, preferred_element_type=jnp.float32) + jnp.dot(grad_value, w_value.T, preferred_element_type=jnp.float32)
    scaled_grad = grad_normed * norm_gain[None, :]
    total_dot = lax.optimization_barrier(jnp.sum(scaled_grad * residual, axis=1))
    grad_input = (out_grad.astype(jnp.float32) + inverse[:, None] * scaled_grad - residual * (inverse ** 3 * total_dot / D)[:, None]).astype(jnp.bfloat16)
    grad_gain = lax.optimization_barrier(jnp.sum(grad_normed * residual * inverse[:, None], axis=0))
    return (layer_out, grad_input, grad_gain, grad_wq, grad_wk, grad_wv, grad_wo)
```

```python
import jax
import jax.numpy as jnp
from jax import lax
from jax.sharding import PartitionSpec as P
from jax.experimental import pallas as pl

D = 8192
H = 64
KV = 8
HD = 128


epsilon = 1e-05
softcap = 20.0
rope_base = 500000.0


def rotary_tables(positions, head_size):
    half_size = head_size // 2
    frequency = rope_base ** (-(jnp.arange(half_size, dtype=jnp.float32) * 2.0) / head_size)
    angles = positions.astype(jnp.float32)[:, None] * frequency[None, :]
    return (jnp.cos(angles), jnp.sin(angles))


def rotate_pairs(values, cosines, sines):
    half_size = values.shape[-1] // 2
    first_half = values[..., :half_size]
    second_half = values[..., half_size:]
    cos_part = cosines[:, None, :]
    sin_part = sines[:, None, :]
    return jnp.concatenate(
        [
            first_half * cos_part - second_half * sin_part,
            second_half * cos_part + first_half * sin_part,
        ],
        axis=-1,
    )


def rotate_back(values, cosines, sines):
    half_size = values.shape[-1] // 2
    first_half = values[..., :half_size]
    second_half = values[..., half_size:]
    cos_part = cosines[:, None, :]
    sin_part = sines[:, None, :]
    return jnp.concatenate(
        [
            first_half * cos_part + second_half * sin_part,
            second_half * cos_part - first_half * sin_part,
        ],
        axis=-1,
    )


def rope_round(values, positions):
    cosines, sines = rotary_tables(positions, HD)
    row_total = values.shape[0]
    return (
        rotate_pairs(values.reshape(row_total, -1, HD), cosines, sines)
        .reshape(row_total, -1)
        .astype(jnp.bfloat16)
    )


def to_blocks(values, n_row, n_seq):
    length, width = values.shape
    return values.reshape(n_row, length // n_row, n_seq, width // n_seq).transpose(0, 2, 1, 3)


def from_blocks(blocks):
    n_row, n_seq, rows, w = blocks.shape
    return blocks.transpose(0, 2, 1, 3).reshape(n_row * rows, n_seq * w)


def project_kernel(lhs_ref, wq_ref, wkv_ref, wo_ref, out_ref):
    feat = wq_ref.shape[0]
    qw = wq_ref.shape[1]
    kw = wkv_ref.shape[1]
    ow = wo_ref.shape[0]
    emb = lhs_ref[:, :feat]
    og = lhs_ref[:, feat:]
    out_ref[:, :qw] = jnp.dot(emb, wq_ref[...], preferred_element_type=jnp.float32)
    out_ref[:, qw : qw + kw] = jnp.dot(emb, wkv_ref[...], preferred_element_type=jnp.float32)
    out_ref[:, qw + kw : qw + kw + ow] = lax.dot_general(
        og, wo_ref[...], (((1,), (1,)), ((), ())), preferred_element_type=jnp.float32
    )
    emb_f = emb.astype(jnp.float32)
    squares = jnp.sum(emb_f * emb_f, axis=1, keepdims=True)
    out_ref[:, qw + kw + ow :] = jnp.broadcast_to(
        squares, (squares.shape[0], out_ref.shape[1] - qw - kw - ow)
    )


def project_blocks(lhs, wq, wkv, wo, n_row, n_seq, out_w):
    length, lw = lhs.shape
    feat = wq.shape[0]
    qw = wq.shape[1] // n_seq
    kw = HD
    ow = wo.shape[0] // n_seq
    rows = length // n_row
    flops = 2 * length * feat * (n_seq * (qw + kw + ow))
    return pl.pallas_call(
        project_kernel,
        grid=(n_row, n_seq),
        in_specs=[
            pl.BlockSpec((rows, lw), lambda r, s: (r, 0)),
            pl.BlockSpec((feat, qw), lambda r, s: (0, s)),
            pl.BlockSpec((feat, kw), lambda r, s: (0, s % 2)),
            pl.BlockSpec((ow, feat), lambda r, s: (s, 0)),
        ],
        out_specs=pl.BlockSpec((rows, out_w), lambda r, s: (r * n_seq + s, 0)),
        out_shape=jax.ShapeDtypeStruct((n_row * n_seq * rows, out_w), jnp.float32),
        cost_estimate=pl.CostEstimate(
            flops=flops,
            transcendentals=0,
            bytes_accessed=lhs.size * 2 + (wq.size + wkv.size + wo.size) * 2
            + n_row * n_seq * rows * out_w * 4,
        ),
    )(lhs, wq, wkv, wo)


def per_device(
    motion_ids,
    audio_ids,
    segment_ids,
    motion_table,
    audio_table,
    norm_gain,
    w_query,
    w_key,
    w_value,
    w_out,
    out_grad,
):
    seq_len = segment_ids.shape[0]
    n_row = lax.axis_size("row")
    n_seq = lax.axis_size("seq")
    n_col = lax.axis_size("col")
    row_index = lax.axis_index("row")
    seq_index = lax.axis_index("seq")
    col_index = lax.axis_index("col")
    n_rs = n_row * n_seq
    block_len = seq_len // n_rs
    quarter_len = seq_len // n_row
    own_len = seq_len // n_col
    feat = motion_table.shape[1]
    query_width = w_query.shape[1]
    kv_width = w_key.shape[1]
    head_count = query_width // HD // n_seq
    part_w = head_count * HD
    score_scale = HD ** (-0.5)
    assert kv_width == HD and part_w == 2 * HD

    embedded = (
        jnp.take(motion_table, motion_ids, axis=0).astype(jnp.float32)
        + jnp.take(audio_table, audio_ids, axis=0).astype(jnp.float32)
    ).astype(jnp.bfloat16)
    residual = embedded.astype(jnp.float32)

    both_all = lax.all_gather(
        jnp.concatenate([embedded, out_grad], axis=1), "col", axis=0, tiled=True
    )
    emb_all = both_all[:, :feat]
    grad_all = both_all[:, feat:]
    emb_all_f = emb_all.astype(jnp.float32)
    gain_col = norm_gain[:, None]
    wq_gain = (w_query.astype(jnp.float32) * gain_col).astype(jnp.bfloat16)
    wkv_gain = (
        jnp.concatenate([w_key, w_value], axis=1).astype(jnp.float32) * gain_col
    ).astype(jnp.bfloat16)
    out_w = part_w + HD + part_w + 128
    blocks = project_blocks(both_all, wq_gain, wkv_gain, w_out, n_row, n_seq, out_w)
    got = lax.psum_scatter(blocks, ("row", "seq"), scatter_dimension=0, tiled=True)

    q_raw = got[:, :part_w]
    kv_raw = got[:, part_w : part_w + HD]
    d_raw = got[:, part_w + HD : 2 * part_w + HD]
    sq_q = got[:, 2 * part_w + HD]
    inv_q = lax.rsqrt(sq_q / D + epsilon)

    query_pos = row_index * quarter_len + jnp.arange(quarter_len, dtype=jnp.int32)
    queries = rope_round(q_raw * inv_q[:, None], query_pos)
    kv_scaled = kv_raw * inv_q[:, None]
    kv_piece = jnp.where(
        seq_index % 2 == 0, rope_round(kv_scaled, query_pos), kv_scaled.astype(jnp.bfloat16)
    )
    out_heads = d_raw.astype(jnp.bfloat16).reshape(quarter_len, head_count, HD)

    kv_gath = lax.all_gather(kv_piece, ("row", "seq"), axis=0, tiled=True).reshape(
        n_row, n_seq, quarter_len, HD
    )
    key_sel = kv_gath[:, 0].reshape(seq_len, HD)
    value_sel = kv_gath[:, 1].reshape(seq_len, HD)

    key_pos = jnp.arange(seq_len, dtype=jnp.int32)
    allowed = (key_pos[None, :] <= query_pos[:, None]) & (
        segment_ids[None, :] == jnp.take(segment_ids, query_pos)[:, None]
    )
    query_heads = queries.reshape(quarter_len, head_count, HD)
    raw_scores = (
        jnp.einsum("qhd,kd->hqk", query_heads, key_sel, preferred_element_type=jnp.float32)
        * score_scale
    )
    capped = softcap * jnp.tanh(raw_scores / softcap)
    weights = jnp.where(allowed[None], jnp.exp(capped), 0.0)
    totals = jnp.sum(weights, axis=2)
    attended = jnp.einsum(
        "hqk,kd->qhd", weights.astype(jnp.bfloat16), value_sel, preferred_element_type=jnp.float32
    )
    attn_out = (
        (attended / totals.T[:, :, None]).astype(jnp.bfloat16).reshape(quarter_len, part_w)
    )
    attn_probs = weights / totals[:, :, None]
    prob_grads = jnp.einsum(
        "qhd,kd->hqk", out_heads, value_sel, preferred_element_type=jnp.float32
    )
    row_dots = jnp.sum(attn_probs * prob_grads, axis=2, keepdims=True)
    grad_scores = (
        attn_probs * (prob_grads - row_dots) * (1.0 - (capped / softcap) ** 2) * score_scale
    ).astype(jnp.bfloat16)
    grad_query = jnp.einsum(
        "hqk,kd->qhd", grad_scores, key_sel, preferred_element_type=jnp.float32
    )
    grad_key_part = jnp.einsum(
        "hqk,qhd->kd", grad_scores, query_heads, preferred_element_type=jnp.float32
    )
    grad_value_part = jnp.einsum(
        "hqk,qhd->kd",
        attn_probs.astype(jnp.bfloat16),
        out_heads,
        preferred_element_type=jnp.float32,
    )
    cos_all, sin_all = rotary_tables(key_pos, HD)
    grad_key_rot = rotate_back(grad_key_part[:, None, :], cos_all, sin_all).reshape(
        seq_len, kv_width
    )
    kv_grad_sum = lax.psum_scatter(
        jnp.concatenate([grad_key_rot, grad_value_part], axis=1),
        ("row", "seq"),
        scatter_dimension=0,
        tiled=True,
    ).astype(jnp.bfloat16)
    cos_query, sin_query = rotary_tables(query_pos, HD)
    grad_query_round = (
        rotate_back(grad_query, cos_query, sin_query)
        .reshape(quarter_len, part_w)
        .astype(jnp.bfloat16)
    )
    inv_hi = inv_q.astype(jnp.bfloat16)
    inv_lo = (inv_q - inv_hi.astype(jnp.float32)).astype(jnp.bfloat16)
    inv_rows = -(-2 * quarter_len // part_w)
    inv_rows = inv_rows + (-inv_rows) % 8
    inv_pack = jnp.pad(
        jnp.concatenate([inv_hi, inv_lo]), (0, inv_rows * part_w - 2 * quarter_len)
    ).reshape(inv_rows, part_w)
    back_rows = 2 * quarter_len + block_len + inv_rows
    back_all = lax.all_gather(
        jnp.concatenate([attn_out, grad_query_round, kv_grad_sum, inv_pack], axis=0),
        ("row", "seq"),
        axis=0,
        tiled=True,
    ).reshape(n_rs, back_rows, part_w)
    inv_parts = back_all[:, 2 * quarter_len + block_len :].reshape(n_rs, -1)
    inv_blocks = inv_parts[:, :quarter_len].astype(jnp.float32) + inv_parts[
        :, quarter_len : 2 * quarter_len
    ].astype(jnp.float32)
    inv_all = inv_blocks.reshape(n_row, n_seq, quarter_len)[:, 0].reshape(seq_len)
    out_all = from_blocks(back_all[:, :quarter_len].reshape(n_row, n_seq, quarter_len, part_w))
    grad_query_all = from_blocks(
        back_all[:, quarter_len : 2 * quarter_len].reshape(n_row, n_seq, quarter_len, part_w)
    )
    kv_grad_all = back_all[:, 2 * quarter_len : 2 * quarter_len + block_len].reshape(
        seq_len, part_w
    )

    normed_all = (emb_all_f * inv_all[:, None] * norm_gain[None, :]).astype(jnp.bfloat16)
    grad_wo = jnp.einsum("ln,ld->nd", out_all, grad_all, preferred_element_type=jnp.float32)
    grad_wq = jnp.einsum(
        "ld,ln->dn", normed_all, grad_query_all, preferred_element_type=jnp.float32
    )
    grad_wk = jnp.einsum(
        "ld,ln->dn", normed_all, kv_grad_all[:, :kv_width], preferred_element_type=jnp.float32
    )
    grad_wv = jnp.einsum(
        "ld,ln->dn", normed_all, kv_grad_all[:, kv_width:], preferred_element_type=jnp.float32
    )

    branch_part = jnp.dot(out_all, w_out, preferred_element_type=jnp.float32)
    total_term = jnp.einsum(
        "ln,dn->ld", grad_query_all, w_query, preferred_element_type=jnp.float32
    )
    total_term = total_term + jnp.einsum(
        "ln,dn->ld", kv_grad_all[:, :kv_width], w_key, preferred_element_type=jnp.float32
    )
    total_term = total_term + jnp.einsum(
        "ln,dn->ld", kv_grad_all[:, kv_width:], w_value, preferred_element_type=jnp.float32
    )
    col_sum = lax.psum_scatter(
        jnp.concatenate([branch_part, total_term], axis=1).astype(jnp.bfloat16),
        "col",
        scatter_dimension=0,
        tiled=True,
    ).astype(jnp.float32)
    branch_sum = col_sum[:, :feat]
    grad_normed = col_sum[:, feat:]
    layer_out = (residual + branch_sum).astype(jnp.bfloat16)

    inverse = lax.dynamic_slice(inv_all, (col_index * own_len,), (own_len,))
    scaled_grad = grad_normed * norm_gain[None, :]
    total_dot = lax.psum(lax.psum(jnp.sum(scaled_grad * residual, axis=1), "seq"), "row")
    grad_input = (
        out_grad.astype(jnp.float32)
        + inverse[:, None] * scaled_grad
        - residual * (inverse**3 * total_dot / D)[:, None]
    ).astype(jnp.bfloat16)
    grad_gain = lax.psum(jnp.sum(grad_normed * residual * inverse[:, None], axis=0), "col")
    return (layer_out, grad_input, grad_gain, grad_wq, grad_wk, grad_wv, grad_wo)


def solution(mesh):
    placed = (
        P("col"),
        P("col"),
        P(),
        P(None, ("row", "seq")),
        P(None, ("row", "seq")),
        P(("row", "seq")),
        P(("row", "seq"), "col"),
        P(("row", "seq"), "col"),
        P(("row", "seq"), "col"),
        P("col", ("row", "seq")),
        P("col", ("row", "seq")),
    )
    return jax.shard_map(
        per_device,
        mesh=mesh,
        in_specs=placed,
        out_specs=(
            P("col", ("row", "seq")),
            P("col", ("row", "seq")),
            P(("row", "seq")),
            P(("row", "seq"), "col"),
            P(("row", "seq"), "col"),
            P(("row", "seq"), "col"),
            P("col", ("row", "seq")),
        ),
        check_vma=False,
    )
```

```python
import jax
import jax.numpy as jnp
from jax import lax
from jax.sharding import PartitionSpec as P
from jax.experimental import pallas as pl

D = 8192
H = 64
KV = 8
HD = 128


epsilon = 1e-05
softcap = 20.0
rope_base = 500000.0
MAX_DOC = 768


def rotary_tables(positions, head_size):
    half_size = head_size // 2
    frequency = rope_base ** (-(jnp.arange(half_size, dtype=jnp.float32) * 2.0) / head_size)
    angles = positions.astype(jnp.float32)[:, None] * frequency[None, :]
    return (jnp.cos(angles), jnp.sin(angles))


def rotate_pairs(values, cosines, sines):
    half_size = values.shape[-1] // 2
    first_half = values[..., :half_size]
    second_half = values[..., half_size:]
    cos_part = cosines[:, None, :]
    sin_part = sines[:, None, :]
    return jnp.concatenate(
        [
            first_half * cos_part - second_half * sin_part,
            second_half * cos_part + first_half * sin_part,
        ],
        axis=-1,
    )


def rotate_back(values, cosines, sines):
    half_size = values.shape[-1] // 2
    first_half = values[..., :half_size]
    second_half = values[..., half_size:]
    cos_part = cosines[:, None, :]
    sin_part = sines[:, None, :]
    return jnp.concatenate(
        [
            first_half * cos_part + second_half * sin_part,
            second_half * cos_part - first_half * sin_part,
        ],
        axis=-1,
    )


def rope_round(values, positions):
    cosines, sines = rotary_tables(positions, HD)
    row_total = values.shape[0]
    return (
        rotate_pairs(values.reshape(row_total, -1, HD), cosines, sines)
        .reshape(row_total, -1)
        .astype(jnp.bfloat16)
    )


def to_blocks(values, n_row, n_seq):
    length, width = values.shape
    return values.reshape(n_row, length // n_row, n_seq, width // n_seq).transpose(0, 2, 1, 3)


def from_blocks(blocks):
    n_row, n_seq, rows, w = blocks.shape
    return blocks.transpose(0, 2, 1, 3).reshape(n_row * rows, n_seq * w)


def project_kernel(lhs_ref, wq_ref, wkv_ref, wo_ref, out_ref):
    feat = wq_ref.shape[0]
    qw = wq_ref.shape[1]
    kw = wkv_ref.shape[1]
    ow = wo_ref.shape[0]
    emb = lhs_ref[:, :feat]
    og = lhs_ref[:, feat:]
    out_ref[:, :qw] = jnp.dot(emb, wq_ref[...], preferred_element_type=jnp.float32)
    out_ref[:, qw : qw + kw] = jnp.dot(emb, wkv_ref[...], preferred_element_type=jnp.float32)
    out_ref[:, qw + kw : qw + kw + ow] = lax.dot_general(
        og, wo_ref[...], (((1,), (1,)), ((), ())), preferred_element_type=jnp.float32
    )
    emb_f = emb.astype(jnp.float32)
    squares = jnp.sum(emb_f * emb_f, axis=1, keepdims=True)
    out_ref[:, qw + kw + ow :] = jnp.broadcast_to(
        squares, (squares.shape[0], out_ref.shape[1] - qw - kw - ow)
    )


def project_blocks(lhs, wq, wkv, wo, n_row, n_seq, out_w):
    length, lw = lhs.shape
    feat = wq.shape[0]
    qw = wq.shape[1] // n_seq
    kw = HD
    ow = wo.shape[0] // n_seq
    rows = length // n_row
    flops = 2 * length * feat * (n_seq * (qw + kw + ow))
    return pl.pallas_call(
        project_kernel,
        grid=(n_row, n_seq),
        in_specs=[
            pl.BlockSpec((rows, lw), lambda r, s: (r, 0)),
            pl.BlockSpec((feat, qw), lambda r, s: (0, s)),
            pl.BlockSpec((feat, kw), lambda r, s: (0, s % 2)),
            pl.BlockSpec((ow, feat), lambda r, s: (s, 0)),
        ],
        out_specs=pl.BlockSpec((rows, out_w), lambda r, s: (r * n_seq + s, 0)),
        out_shape=jax.ShapeDtypeStruct((n_row * n_seq * rows, out_w), jnp.float32),
        cost_estimate=pl.CostEstimate(
            flops=flops,
            transcendentals=0,
            bytes_accessed=lhs.size * 2 + (wq.size + wkv.size + wo.size) * 2
            + n_row * n_seq * rows * out_w * 4,
        ),
    )(lhs, wq, wkv, wo)


def per_device(
    motion_ids,
    audio_ids,
    segment_ids,
    motion_table,
    audio_table,
    norm_gain,
    w_query,
    w_key,
    w_value,
    w_out,
    out_grad,
):
    seq_len = segment_ids.shape[0]
    n_row = lax.axis_size("row")
    n_seq = lax.axis_size("seq")
    n_col = lax.axis_size("col")
    row_index = lax.axis_index("row")
    seq_index = lax.axis_index("seq")
    col_index = lax.axis_index("col")
    n_rs = n_row * n_seq
    block_len = seq_len // n_rs
    quarter_len = seq_len // n_row
    own_len = seq_len // n_col
    feat = motion_table.shape[1]
    query_width = w_query.shape[1]
    kv_width = w_key.shape[1]
    head_count = query_width // HD // n_seq
    part_w = head_count * HD
    score_scale = HD ** (-0.5)
    assert kv_width == HD and part_w == 2 * HD

    embedded = (
        jnp.take(motion_table, motion_ids, axis=0).astype(jnp.float32)
        + jnp.take(audio_table, audio_ids, axis=0).astype(jnp.float32)
    ).astype(jnp.bfloat16)
    residual = embedded.astype(jnp.float32)

    both_all = lax.all_gather(
        jnp.concatenate([embedded, out_grad], axis=1), "col", axis=0, tiled=True
    )
    emb_all = both_all[:, :feat]
    grad_all = both_all[:, feat:]
    emb_all_f = emb_all.astype(jnp.float32)
    gain_col = norm_gain[:, None]
    wq_gain = (w_query.astype(jnp.float32) * gain_col).astype(jnp.bfloat16)
    wkv_gain = (
        jnp.concatenate([w_key, w_value], axis=1).astype(jnp.float32) * gain_col
    ).astype(jnp.bfloat16)
    out_w = part_w + HD + part_w + 128
    blocks = project_blocks(both_all, wq_gain, wkv_gain, w_out, n_row, n_seq, out_w)
    got = lax.psum_scatter(blocks, ("row", "seq"), scatter_dimension=0, tiled=True)

    q_raw = got[:, :part_w]
    kv_raw = got[:, part_w : part_w + HD]
    d_raw = got[:, part_w + HD : 2 * part_w + HD]
    sq_q = got[:, 2 * part_w + HD]
    inv_q = lax.rsqrt(sq_q / D + epsilon)

    query_pos = row_index * quarter_len + jnp.arange(quarter_len, dtype=jnp.int32)
    queries = rope_round(q_raw * inv_q[:, None], query_pos)
    kv_scaled = kv_raw * inv_q[:, None]
    kv_piece = jnp.where(
        seq_index % 2 == 0, rope_round(kv_scaled, query_pos), kv_scaled.astype(jnp.bfloat16)
    )
    out_heads = d_raw.astype(jnp.bfloat16).reshape(quarter_len, head_count, HD)

    kv_gath = lax.all_gather(kv_piece, ("row", "seq"), axis=0, tiled=True).reshape(
        n_row, n_seq, quarter_len, HD
    )
    key_all = kv_gath[:, 0].reshape(seq_len, HD)
    value_all = kv_gath[:, 1].reshape(seq_len, HD)

    doc_back = -(-(MAX_DOC - 1) // quarter_len) * quarter_len
    win = min(seq_len, quarter_len + doc_back)
    win_start = jnp.clip(row_index * quarter_len - doc_back, 0, seq_len - win)
    key_pos = win_start + jnp.arange(win, dtype=jnp.int32)
    key_sel = lax.dynamic_slice(key_all, (win_start, 0), (win, HD))
    value_sel = lax.dynamic_slice(value_all, (win_start, 0), (win, HD))
    key_seg = lax.dynamic_slice(segment_ids, (win_start,), (win,))
    allowed = (key_pos[None, :] <= query_pos[:, None]) & (
        key_seg[None, :] == jnp.take(segment_ids, query_pos)[:, None]
    )
    query_heads = queries.reshape(quarter_len, head_count, HD)
    raw_scores = (
        jnp.einsum("qhd,kd->hqk", query_heads, key_sel, preferred_element_type=jnp.float32)
        * score_scale
    )
    capped = softcap * jnp.tanh(raw_scores / softcap)
    weights = jnp.where(allowed[None], jnp.exp(capped), 0.0)
    totals = jnp.sum(weights, axis=2)
    attended = jnp.einsum(
        "hqk,kd->qhd", weights.astype(jnp.bfloat16), value_sel, preferred_element_type=jnp.float32
    )
    attn_out = (
        (attended / totals.T[:, :, None]).astype(jnp.bfloat16).reshape(quarter_len, part_w)
    )
    attn_probs = weights / totals[:, :, None]
    prob_grads = jnp.einsum(
        "qhd,kd->hqk", out_heads, value_sel, preferred_element_type=jnp.float32
    )
    row_dots = jnp.sum(attn_probs * prob_grads, axis=2, keepdims=True)
    grad_scores = (
        attn_probs * (prob_grads - row_dots) * (1.0 - (capped / softcap) ** 2) * score_scale
    ).astype(jnp.bfloat16)
    grad_query = jnp.einsum(
        "hqk,kd->qhd", grad_scores, key_sel, preferred_element_type=jnp.float32
    )
    grad_key_part = jnp.einsum(
        "hqk,qhd->kd", grad_scores, query_heads, preferred_element_type=jnp.float32
    )
    grad_value_part = jnp.einsum(
        "hqk,qhd->kd",
        attn_probs.astype(jnp.bfloat16),
        out_heads,
        preferred_element_type=jnp.float32,
    )
    cos_all, sin_all = rotary_tables(key_pos, HD)
    grad_key_rot = rotate_back(grad_key_part[:, None, :], cos_all, sin_all).reshape(
        win, kv_width
    )
    kv_grad_win = jnp.concatenate([grad_key_rot, grad_value_part], axis=1).astype(jnp.bfloat16)
    cos_query, sin_query = rotary_tables(query_pos, HD)
    grad_query_round = (
        rotate_back(grad_query, cos_query, sin_query)
        .reshape(quarter_len, part_w)
        .astype(jnp.bfloat16)
    )
    inv_hi = inv_q.astype(jnp.bfloat16)
    inv_lo = (inv_q - inv_hi.astype(jnp.float32)).astype(jnp.bfloat16)
    inv_rows = -(-2 * quarter_len // part_w)
    inv_rows = inv_rows + (-inv_rows) % 8
    inv_pack = jnp.pad(
        jnp.concatenate([inv_hi, inv_lo]), (0, inv_rows * part_w - 2 * quarter_len)
    ).reshape(inv_rows, part_w)
    back_rows = 2 * quarter_len + win + inv_rows
    back_all = lax.all_gather(
        jnp.concatenate([attn_out, grad_query_round, kv_grad_win, inv_pack], axis=0),
        ("row", "seq"),
        axis=0,
        tiled=True,
    ).reshape(n_rs, back_rows, part_w)
    inv_parts = back_all[:, 2 * quarter_len + win :].reshape(n_rs, -1)
    inv_blocks = inv_parts[:, :quarter_len].astype(jnp.float32) + inv_parts[
        :, quarter_len : 2 * quarter_len
    ].astype(jnp.float32)
    inv_all = inv_blocks.reshape(n_row, n_seq, quarter_len)[:, 0].reshape(seq_len)
    out_all = from_blocks(back_all[:, :quarter_len].reshape(n_row, n_seq, quarter_len, part_w))
    grad_query_all = from_blocks(
        back_all[:, quarter_len : 2 * quarter_len].reshape(n_row, n_seq, quarter_len, part_w)
    )
    kv_terms = (
        back_all[:, 2 * quarter_len : 2 * quarter_len + win]
        .astype(jnp.float32)
        .reshape(n_row, n_seq, win, part_w)
        .sum(axis=1)
    )
    kv_grad_f = jnp.zeros((seq_len, part_w), jnp.float32)
    for quarter in range(n_row):
        first = min(max(quarter * quarter_len - doc_back, 0), seq_len - win)
        kv_grad_f = kv_grad_f.at[first : first + win].add(kv_terms[quarter])
    kv_grad_all = kv_grad_f.astype(jnp.bfloat16)

    normed_all = (emb_all_f * inv_all[:, None] * norm_gain[None, :]).astype(jnp.bfloat16)
    grad_wo = jnp.einsum("ln,ld->nd", out_all, grad_all, preferred_element_type=jnp.float32)
    grad_wq = jnp.einsum(
        "ld,ln->dn", normed_all, grad_query_all, preferred_element_type=jnp.float32
    )
    grad_wk = jnp.einsum(
        "ld,ln->dn", normed_all, kv_grad_all[:, :kv_width], preferred_element_type=jnp.float32
    )
    grad_wv = jnp.einsum(
        "ld,ln->dn", normed_all, kv_grad_all[:, kv_width:], preferred_element_type=jnp.float32
    )

    branch_part = jnp.dot(out_all, w_out, preferred_element_type=jnp.float32)
    total_term = jnp.einsum(
        "ln,dn->ld", grad_query_all, w_query, preferred_element_type=jnp.float32
    )
    total_term = total_term + jnp.einsum(
        "ln,dn->ld", kv_grad_all[:, :kv_width], w_key, preferred_element_type=jnp.float32
    )
    total_term = total_term + jnp.einsum(
        "ln,dn->ld", kv_grad_all[:, kv_width:], w_value, preferred_element_type=jnp.float32
    )
    col_sum = lax.psum_scatter(
        jnp.concatenate([branch_part, total_term], axis=1).astype(jnp.bfloat16),
        "col",
        scatter_dimension=0,
        tiled=True,
    ).astype(jnp.float32)
    branch_sum = col_sum[:, :feat]
    grad_normed = col_sum[:, feat:]
    layer_out = (residual + branch_sum).astype(jnp.bfloat16)

    inverse = lax.dynamic_slice(inv_all, (col_index * own_len,), (own_len,))
    scaled_grad = grad_normed * norm_gain[None, :]
    total_dot = lax.psum(lax.psum(jnp.sum(scaled_grad * residual, axis=1), "seq"), "row")
    grad_input = (
        out_grad.astype(jnp.float32)
        + inverse[:, None] * scaled_grad
        - residual * (inverse**3 * total_dot / D)[:, None]
    ).astype(jnp.bfloat16)
    grad_gain = lax.psum(jnp.sum(grad_normed * residual * inverse[:, None], axis=0), "col")
    return (layer_out, grad_input, grad_gain, grad_wq, grad_wk, grad_wv, grad_wo)


def solution(mesh):
    placed = (
        P("col"),
        P("col"),
        P(),
        P(None, ("row", "seq")),
        P(None, ("row", "seq")),
        P(("row", "seq")),
        P(("row", "seq"), "col"),
        P(("row", "seq"), "col"),
        P(("row", "seq"), "col"),
        P("col", ("row", "seq")),
        P("col", ("row", "seq")),
    )
    return jax.shard_map(
        per_device,
        mesh=mesh,
        in_specs=placed,
        out_specs=(
            P("col", ("row", "seq")),
            P("col", ("row", "seq")),
            P(("row", "seq")),
            P(("row", "seq"), "col"),
            P(("row", "seq"), "col"),
            P(("row", "seq"), "col"),
            P("col", ("row", "seq")),
        ),
        check_vma=False,
    )
```

```python
import jax
import jax.numpy as jnp
from jax import lax
from jax.sharding import PartitionSpec as P
from jax.experimental import pallas as pl

D = 8192
H = 64
KV = 8
HD = 128


epsilon = 1e-05
softcap = 20.0
rope_base = 500000.0
MAX_DOC = 768


def rotary_tables(positions, head_size):
    half_size = head_size // 2
    frequency = rope_base ** (-(jnp.arange(half_size, dtype=jnp.float32) * 2.0) / head_size)
    angles = positions.astype(jnp.float32)[:, None] * frequency[None, :]
    return (jnp.cos(angles), jnp.sin(angles))


def rotate_pairs(values, cosines, sines):
    half_size = values.shape[-1] // 2
    first_half = values[..., :half_size]
    second_half = values[..., half_size:]
    cos_part = cosines[:, None, :]
    sin_part = sines[:, None, :]
    return jnp.concatenate(
        [
            first_half * cos_part - second_half * sin_part,
            second_half * cos_part + first_half * sin_part,
        ],
        axis=-1,
    )


def rotate_back(values, cosines, sines):
    half_size = values.shape[-1] // 2
    first_half = values[..., :half_size]
    second_half = values[..., half_size:]
    cos_part = cosines[:, None, :]
    sin_part = sines[:, None, :]
    return jnp.concatenate(
        [
            first_half * cos_part + second_half * sin_part,
            second_half * cos_part - first_half * sin_part,
        ],
        axis=-1,
    )


def rope_round(values, positions):
    cosines, sines = rotary_tables(positions, HD)
    row_total = values.shape[0]
    return (
        rotate_pairs(values.reshape(row_total, -1, HD), cosines, sines)
        .reshape(row_total, -1)
        .astype(jnp.bfloat16)
    )


def to_blocks(values, n_row, n_seq):
    length, width = values.shape
    return values.reshape(n_row, length // n_row, n_seq, width // n_seq).transpose(0, 2, 1, 3)


def from_blocks(blocks):
    n_row, n_seq, rows, w = blocks.shape
    return blocks.transpose(0, 2, 1, 3).reshape(n_row * rows, n_seq * w)


def project_kernel(lhs_ref, wq_ref, wkv_ref, wo_ref, out_ref):
    feat = wq_ref.shape[0]
    qw = wq_ref.shape[1]
    kw = wkv_ref.shape[1]
    ow = wo_ref.shape[0]
    emb = lhs_ref[:, :feat]
    og = lhs_ref[:, feat:]
    out_ref[:, :qw] = jnp.dot(emb, wq_ref[...], preferred_element_type=jnp.float32)
    out_ref[:, qw : qw + kw] = jnp.dot(emb, wkv_ref[...], preferred_element_type=jnp.float32)
    out_ref[:, qw + kw : qw + kw + ow] = lax.dot_general(
        og, wo_ref[...], (((1,), (1,)), ((), ())), preferred_element_type=jnp.float32
    )
    emb_f = emb.astype(jnp.float32)
    squares = jnp.sum(emb_f * emb_f, axis=1, keepdims=True)
    out_ref[:, qw + kw + ow :] = jnp.broadcast_to(
        squares, (squares.shape[0], out_ref.shape[1] - qw - kw - ow)
    )


def project_blocks(lhs, wq, wkv, wo, n_row, n_seq, out_w):
    length, lw = lhs.shape
    feat = wq.shape[0]
    qw = wq.shape[1] // n_seq
    kw = HD
    ow = wo.shape[0] // n_seq
    rows = length // n_row
    flops = 2 * length * feat * (n_seq * (qw + kw + ow))
    return pl.pallas_call(
        project_kernel,
        grid=(n_row, n_seq),
        in_specs=[
            pl.BlockSpec((rows, lw), lambda r, s: (r, 0)),
            pl.BlockSpec((feat, qw), lambda r, s: (0, s)),
            pl.BlockSpec((feat, kw), lambda r, s: (0, s % 2)),
            pl.BlockSpec((ow, feat), lambda r, s: (s, 0)),
        ],
        out_specs=pl.BlockSpec((rows, out_w), lambda r, s: (r * n_seq + s, 0)),
        out_shape=jax.ShapeDtypeStruct((n_row * n_seq * rows, out_w), jnp.float32),
        cost_estimate=pl.CostEstimate(
            flops=flops,
            transcendentals=0,
            bytes_accessed=lhs.size * 2 + (wq.size + wkv.size + wo.size) * 2
            + n_row * n_seq * rows * out_w * 4,
        ),
    )(lhs, wq, wkv, wo)


def per_device(
    motion_ids,
    audio_ids,
    segment_ids,
    motion_table,
    audio_table,
    norm_gain,
    w_query,
    w_key,
    w_value,
    w_out,
    out_grad,
):
    seq_len = segment_ids.shape[0]
    n_row = lax.axis_size("row")
    n_seq = lax.axis_size("seq")
    n_col = lax.axis_size("col")
    row_index = lax.axis_index("row")
    seq_index = lax.axis_index("seq")
    col_index = lax.axis_index("col")
    n_rs = n_row * n_seq
    block_len = seq_len // n_rs
    quarter_len = seq_len // n_row
    own_len = seq_len // n_col
    feat = motion_table.shape[1]
    query_width = w_query.shape[1]
    kv_width = w_key.shape[1]
    head_count = query_width // HD // n_seq
    part_w = head_count * HD
    score_scale = HD ** (-0.5)
    assert kv_width == HD and part_w == 2 * HD

    embedded = (
        jnp.take(motion_table, motion_ids, axis=0).astype(jnp.float32)
        + jnp.take(audio_table, audio_ids, axis=0).astype(jnp.float32)
    ).astype(jnp.bfloat16)
    residual = embedded.astype(jnp.float32)

    both_all = lax.all_gather(
        jnp.concatenate([embedded, out_grad], axis=1), "col", axis=0, tiled=True
    )
    emb_all = both_all[:, :feat]
    grad_all = both_all[:, feat:]
    emb_all_f = emb_all.astype(jnp.float32)
    gain_col = norm_gain[:, None]
    wq_gain = (w_query.astype(jnp.float32) * gain_col).astype(jnp.bfloat16)
    wkv_gain = (
        jnp.concatenate([w_key, w_value], axis=1).astype(jnp.float32) * gain_col
    ).astype(jnp.bfloat16)
    out_w = part_w + HD + part_w + 128
    blocks = project_blocks(both_all, wq_gain, wkv_gain, w_out, n_row, n_seq, out_w)
    got = lax.psum_scatter(blocks, ("row", "seq"), scatter_dimension=0, tiled=True)

    q_raw = got[:, :part_w]
    kv_raw = got[:, part_w : part_w + HD]
    d_raw = got[:, part_w + HD : 2 * part_w + HD]
    sq_q = got[:, 2 * part_w + HD]
    inv_q = lax.rsqrt(sq_q / D + epsilon)

    query_pos = row_index * quarter_len + jnp.arange(quarter_len, dtype=jnp.int32)
    queries = rope_round(q_raw * inv_q[:, None], query_pos)
    kv_scaled = kv_raw * inv_q[:, None]
    kv_piece = jnp.where(
        seq_index % 2 == 0, rope_round(kv_scaled, query_pos), kv_scaled.astype(jnp.bfloat16)
    )
    out_heads = d_raw.astype(jnp.bfloat16).reshape(quarter_len, head_count, HD)

    kv_gath = lax.all_gather(kv_piece, ("row", "seq"), axis=0, tiled=True).reshape(
        n_row, n_seq, quarter_len, HD
    )
    key_all = kv_gath[:, 0].reshape(seq_len, HD)
    value_all = kv_gath[:, 1].reshape(seq_len, HD)

    doc_back = -(-(MAX_DOC - 1) // quarter_len) * quarter_len
    win = min(seq_len, quarter_len + doc_back)
    win_start = jnp.clip(row_index * quarter_len - doc_back, 0, seq_len - win)
    key_pos = win_start + jnp.arange(win, dtype=jnp.int32)
    key_sel = lax.dynamic_slice(key_all, (win_start, 0), (win, HD))
    value_sel = lax.dynamic_slice(value_all, (win_start, 0), (win, HD))
    key_seg = lax.dynamic_slice(segment_ids, (win_start,), (win,))
    allowed = (key_pos[None, :] <= query_pos[:, None]) & (
        key_seg[None, :] == jnp.take(segment_ids, query_pos)[:, None]
    )
    query_heads = queries.reshape(quarter_len, head_count, HD)
    raw_scores = (
        jnp.einsum("qhd,kd->hqk", query_heads, key_sel, preferred_element_type=jnp.float32)
        * score_scale
    )
    capped = softcap * jnp.tanh(raw_scores / softcap)
    weights = jnp.where(allowed[None], jnp.exp(capped), 0.0)
    totals = jnp.sum(weights, axis=2)
    attended = jnp.einsum(
        "hqk,kd->qhd", weights.astype(jnp.bfloat16), value_sel, preferred_element_type=jnp.float32
    )
    attn_out = (
        (attended / totals.T[:, :, None]).astype(jnp.bfloat16).reshape(quarter_len, part_w)
    )
    attn_probs = weights / totals[:, :, None]
    prob_grads = jnp.einsum(
        "qhd,kd->hqk", out_heads, value_sel, preferred_element_type=jnp.float32
    )
    row_dots = jnp.sum(attn_probs * prob_grads, axis=2, keepdims=True)
    grad_scores = (
        attn_probs * (prob_grads - row_dots) * (1.0 - (capped / softcap) ** 2) * score_scale
    ).astype(jnp.bfloat16)
    grad_query = jnp.einsum(
        "hqk,kd->qhd", grad_scores, key_sel, preferred_element_type=jnp.float32
    )
    grad_key_part = jnp.einsum(
        "hqk,qhd->kd", grad_scores, query_heads, preferred_element_type=jnp.float32
    )
    grad_value_part = jnp.einsum(
        "hqk,qhd->kd",
        attn_probs.astype(jnp.bfloat16),
        out_heads,
        preferred_element_type=jnp.float32,
    )
    cos_all, sin_all = rotary_tables(key_pos, HD)
    grad_key_rot = rotate_back(grad_key_part[:, None, :], cos_all, sin_all).reshape(
        win, kv_width
    )
    kv_grad_win = jnp.concatenate([grad_key_rot, grad_value_part], axis=1).astype(jnp.bfloat16)
    cos_query, sin_query = rotary_tables(query_pos, HD)
    grad_query_round = (
        rotate_back(grad_query, cos_query, sin_query)
        .reshape(quarter_len, part_w)
        .astype(jnp.bfloat16)
    )
    inv_hi = inv_q.astype(jnp.bfloat16)
    inv_lo = (inv_q - inv_hi.astype(jnp.float32)).astype(jnp.bfloat16)
    inv_rows = -(-2 * quarter_len // part_w)
    inv_rows = inv_rows + (-inv_rows) % 8
    inv_pack = jnp.pad(
        jnp.concatenate([inv_hi, inv_lo]), (0, inv_rows * part_w - 2 * quarter_len)
    ).reshape(inv_rows, part_w)
    back_rows = 2 * quarter_len + win + inv_rows
    back_all = lax.all_gather(
        jnp.concatenate([attn_out, grad_query_round, kv_grad_win, inv_pack], axis=0),
        ("row", "seq"),
        axis=0,
        tiled=True,
    ).reshape(n_rs, back_rows, part_w)
    inv_parts = back_all[:, 2 * quarter_len + win :].reshape(n_rs, -1)
    inv_blocks = inv_parts[:, :quarter_len].astype(jnp.float32) + inv_parts[
        :, quarter_len : 2 * quarter_len
    ].astype(jnp.float32)
    inv_all = inv_blocks.reshape(n_row, n_seq, quarter_len)[:, 0].reshape(seq_len)
    out_all = from_blocks(back_all[:, :quarter_len].reshape(n_row, n_seq, quarter_len, part_w))
    grad_query_all = from_blocks(
        back_all[:, quarter_len : 2 * quarter_len].reshape(n_row, n_seq, quarter_len, part_w)
    )
    kv_terms = (
        back_all[:, 2 * quarter_len : 2 * quarter_len + win]
        .astype(jnp.float32)
        .reshape(n_row, n_seq, win, part_w)
        .sum(axis=1)
    )
    kv_grad_f = jnp.zeros((seq_len, part_w), jnp.float32)
    for quarter in range(n_row):
        first = min(max(quarter * quarter_len - doc_back, 0), seq_len - win)
        kv_grad_f = kv_grad_f.at[first : first + win].add(kv_terms[quarter])
    kv_grad_all = kv_grad_f.astype(jnp.bfloat16)

    normed_all = (emb_all_f * inv_all[:, None] * norm_gain[None, :]).astype(jnp.bfloat16)
    grad_wo = jnp.einsum("ln,ld->nd", out_all, grad_all, preferred_element_type=jnp.float32)
    grad_wq = jnp.einsum(
        "ld,ln->dn", normed_all, grad_query_all, preferred_element_type=jnp.float32
    )
    grad_wk = jnp.einsum(
        "ld,ln->dn", normed_all, kv_grad_all[:, :kv_width], preferred_element_type=jnp.float32
    )
    grad_wv = jnp.einsum(
        "ld,ln->dn", normed_all, kv_grad_all[:, kv_width:], preferred_element_type=jnp.float32
    )

    branch_part = jnp.dot(out_all, w_out, preferred_element_type=jnp.float32)
    total_term = jnp.einsum(
        "ln,dn->ld", grad_query_all, w_query, preferred_element_type=jnp.float32
    )
    total_term = total_term + jnp.einsum(
        "ln,dn->ld", kv_grad_all[:, :kv_width], w_key, preferred_element_type=jnp.float32
    )
    total_term = total_term + jnp.einsum(
        "ln,dn->ld", kv_grad_all[:, kv_width:], w_value, preferred_element_type=jnp.float32
    )
    emb_inv_all = emb_all_f * inv_all[:, None]
    gain_terms = jnp.sum(total_term * emb_inv_all, axis=0)
    dot_terms = jnp.sum(total_term * (emb_all_f * norm_gain[None, :]), axis=1)
    col_terms = lax.psum(jnp.concatenate([gain_terms, dot_terms]), "col")
    grad_gain = col_terms[:feat]
    own_dots = lax.dynamic_slice(col_terms[feat:], (col_index * own_len,), (own_len,))
    total_dot = lax.psum(lax.psum(own_dots, "seq"), "row")
    col_sum = lax.psum_scatter(
        jnp.concatenate([branch_part, total_term], axis=1).astype(jnp.bfloat16),
        "col",
        scatter_dimension=0,
        tiled=True,
    ).astype(jnp.float32)
    branch_sum = col_sum[:, :feat]
    grad_normed = col_sum[:, feat:]
    layer_out = (residual + branch_sum).astype(jnp.bfloat16)

    inverse = lax.dynamic_slice(inv_all, (col_index * own_len,), (own_len,))
    scaled_grad = grad_normed * norm_gain[None, :]
    grad_input = (
        out_grad.astype(jnp.float32)
        + inverse[:, None] * scaled_grad
        - residual * (inverse**3 * total_dot / D)[:, None]
    ).astype(jnp.bfloat16)
    return (layer_out, grad_input, grad_gain, grad_wq, grad_wk, grad_wv, grad_wo)


def solution(mesh):
    placed = (
        P("col"),
        P("col"),
        P(),
        P(None, ("row", "seq")),
        P(None, ("row", "seq")),
        P(("row", "seq")),
        P(("row", "seq"), "col"),
        P(("row", "seq"), "col"),
        P(("row", "seq"), "col"),
        P("col", ("row", "seq")),
        P("col", ("row", "seq")),
    )
    return jax.shard_map(
        per_device,
        mesh=mesh,
        in_specs=placed,
        out_specs=(
            P("col", ("row", "seq")),
            P("col", ("row", "seq")),
            P(("row", "seq")),
            P(("row", "seq"), "col"),
            P(("row", "seq"), "col"),
            P(("row", "seq"), "col"),
            P("col", ("row", "seq")),
        ),
        check_vma=False,
    )
```

```python
import jax
import jax.numpy as jnp
from jax import lax
from jax.sharding import PartitionSpec as P
from jax.experimental import pallas as pl

D = 8192
H = 64
KV = 8
HD = 128


epsilon = 1e-05
softcap = 20.0
rope_base = 500000.0
MAX_DOC = 768


def rotary_tables(positions, head_size):
    half_size = head_size // 2
    frequency = rope_base ** (-(jnp.arange(half_size, dtype=jnp.float32) * 2.0) / head_size)
    angles = positions.astype(jnp.float32)[:, None] * frequency[None, :]
    return (jnp.cos(angles), jnp.sin(angles))


def rotate_pairs(values, cosines, sines):
    half_size = values.shape[-1] // 2
    first_half = values[..., :half_size]
    second_half = values[..., half_size:]
    cos_part = cosines[:, None, :]
    sin_part = sines[:, None, :]
    return jnp.concatenate(
        [
            first_half * cos_part - second_half * sin_part,
            second_half * cos_part + first_half * sin_part,
        ],
        axis=-1,
    )


def rotate_back(values, cosines, sines):
    half_size = values.shape[-1] // 2
    first_half = values[..., :half_size]
    second_half = values[..., half_size:]
    cos_part = cosines[:, None, :]
    sin_part = sines[:, None, :]
    return jnp.concatenate(
        [
            first_half * cos_part + second_half * sin_part,
            second_half * cos_part - first_half * sin_part,
        ],
        axis=-1,
    )


def rope_round(values, positions):
    cosines, sines = rotary_tables(positions, HD)
    row_total = values.shape[0]
    return (
        rotate_pairs(values.reshape(row_total, -1, HD), cosines, sines)
        .reshape(row_total, -1)
        .astype(jnp.bfloat16)
    )


def to_blocks(values, n_row, n_seq):
    length, width = values.shape
    return values.reshape(n_row, length // n_row, n_seq, width // n_seq).transpose(0, 2, 1, 3)


def from_blocks(blocks):
    n_row, n_seq, rows, w = blocks.shape
    return blocks.transpose(0, 2, 1, 3).reshape(n_row * rows, n_seq * w)


def project_kernel(lhs_ref, wq_ref, wkv_ref, wo_ref, out_ref):
    feat = wq_ref.shape[0]
    qw = wq_ref.shape[1]
    kw = wkv_ref.shape[1]
    ow = wo_ref.shape[0]
    emb = lhs_ref[:, :feat]
    og = lhs_ref[:, feat:]
    out_ref[:, :qw] = jnp.dot(emb, wq_ref[...], preferred_element_type=jnp.float32)
    out_ref[:, qw : qw + kw] = jnp.dot(emb, wkv_ref[...], preferred_element_type=jnp.float32)
    out_ref[:, qw + kw :] = lax.dot_general(
        og, wo_ref[...], (((1,), (1,)), ((), ())), preferred_element_type=jnp.float32
    )


def project_blocks(lhs, wq, wkv, wo, n_row, n_seq, out_w):
    length, lw = lhs.shape
    feat = wq.shape[0]
    qw = wq.shape[1] // n_seq
    kw = HD
    ow = wo.shape[0] // n_seq
    rows = length // n_row
    flops = 2 * length * feat * (n_seq * (qw + kw + ow))
    return pl.pallas_call(
        project_kernel,
        grid=(n_row, n_seq),
        in_specs=[
            pl.BlockSpec((rows, lw), lambda r, s: (r, 0)),
            pl.BlockSpec((feat, qw), lambda r, s: (0, s)),
            pl.BlockSpec((feat, kw), lambda r, s: (0, s % 2)),
            pl.BlockSpec((ow, feat), lambda r, s: (s, 0)),
        ],
        out_specs=pl.BlockSpec((rows, out_w), lambda r, s: (r * n_seq + s, 0)),
        out_shape=jax.ShapeDtypeStruct((n_row * n_seq * rows, out_w), jnp.float32),
        cost_estimate=pl.CostEstimate(
            flops=flops,
            transcendentals=0,
            bytes_accessed=lhs.size * 2 + (wq.size + wkv.size + wo.size) * 2
            + n_row * n_seq * rows * out_w * 4,
        ),
    )(lhs, wq, wkv, wo)


def per_device(
    motion_ids,
    audio_ids,
    segment_ids,
    motion_table,
    audio_table,
    norm_gain,
    w_query,
    w_key,
    w_value,
    w_out,
    out_grad,
):
    seq_len = segment_ids.shape[0]
    n_row = lax.axis_size("row")
    n_seq = lax.axis_size("seq")
    n_col = lax.axis_size("col")
    row_index = lax.axis_index("row")
    seq_index = lax.axis_index("seq")
    col_index = lax.axis_index("col")
    n_rs = n_row * n_seq
    block_len = seq_len // n_rs
    quarter_len = seq_len // n_row
    own_len = seq_len // n_col
    feat = motion_table.shape[1]
    query_width = w_query.shape[1]
    kv_width = w_key.shape[1]
    head_count = query_width // HD // n_seq
    part_w = head_count * HD
    score_scale = HD ** (-0.5)
    assert kv_width == HD and part_w == 2 * HD

    embedded = (
        jnp.take(motion_table, motion_ids, axis=0).astype(jnp.float32)
        + jnp.take(audio_table, audio_ids, axis=0).astype(jnp.float32)
    ).astype(jnp.bfloat16)
    residual = embedded.astype(jnp.float32)

    both_all = lax.all_gather(
        jnp.concatenate([embedded, out_grad], axis=1), "col", axis=0, tiled=True
    )
    emb_all = both_all[:, :feat]
    grad_all = both_all[:, feat:]
    emb_all_f = emb_all.astype(jnp.float32)
    gain_col = norm_gain[:, None]
    wq_gain = (w_query.astype(jnp.float32) * gain_col).astype(jnp.bfloat16)
    wkv_gain = (
        jnp.concatenate([w_key, w_value], axis=1).astype(jnp.float32) * gain_col
    ).astype(jnp.bfloat16)
    out_w = part_w + HD + part_w
    squares = lax.psum(lax.psum(jnp.sum(emb_all_f * emb_all_f, axis=1), "seq"), "row")
    inv_all = lax.rsqrt(squares / D + epsilon)
    blocks = project_blocks(both_all, wq_gain, wkv_gain, w_out, n_row, n_seq, out_w)
    got = lax.psum_scatter(blocks, ("row", "seq"), scatter_dimension=0, tiled=True)

    q_raw = got[:, :part_w]
    kv_raw = got[:, part_w : part_w + HD]
    d_raw = got[:, part_w + HD : 2 * part_w + HD]
    inv_q = lax.dynamic_slice(inv_all, (row_index * quarter_len,), (quarter_len,))

    query_pos = row_index * quarter_len + jnp.arange(quarter_len, dtype=jnp.int32)
    queries = rope_round(q_raw * inv_q[:, None], query_pos)
    kv_scaled = kv_raw * inv_q[:, None]
    kv_piece = jnp.where(
        seq_index % 2 == 0, rope_round(kv_scaled, query_pos), kv_scaled.astype(jnp.bfloat16)
    )
    out_heads = d_raw.astype(jnp.bfloat16).reshape(quarter_len, head_count, HD)

    kv_gath = lax.all_gather(kv_piece, ("row", "seq"), axis=0, tiled=True).reshape(
        n_row, n_seq, quarter_len, HD
    )
    key_all = kv_gath[:, 0].reshape(seq_len, HD)
    value_all = kv_gath[:, 1].reshape(seq_len, HD)

    doc_back = -(-(MAX_DOC - 1) // quarter_len) * quarter_len
    win = min(seq_len, quarter_len + doc_back)
    win_start = jnp.clip(row_index * quarter_len - doc_back, 0, seq_len - win)
    key_pos = win_start + jnp.arange(win, dtype=jnp.int32)
    key_sel = lax.dynamic_slice(key_all, (win_start, 0), (win, HD))
    value_sel = lax.dynamic_slice(value_all, (win_start, 0), (win, HD))
    key_seg = lax.dynamic_slice(segment_ids, (win_start,), (win,))
    allowed = (key_pos[None, :] <= query_pos[:, None]) & (
        key_seg[None, :] == jnp.take(segment_ids, query_pos)[:, None]
    )
    query_heads = queries.reshape(quarter_len, head_count, HD)
    raw_scores = (
        jnp.einsum("qhd,kd->hqk", query_heads, key_sel, preferred_element_type=jnp.float32)
        * score_scale
    )
    capped = softcap * jnp.tanh(raw_scores / softcap)
    weights = jnp.where(allowed[None], jnp.exp(capped), 0.0)
    totals = jnp.sum(weights, axis=2)
    attended = jnp.einsum(
        "hqk,kd->qhd", weights.astype(jnp.bfloat16), value_sel, preferred_element_type=jnp.float32
    )
    attn_out = (
        (attended / totals.T[:, :, None]).astype(jnp.bfloat16).reshape(quarter_len, part_w)
    )
    attn_probs = weights / totals[:, :, None]
    prob_grads = jnp.einsum(
        "qhd,kd->hqk", out_heads, value_sel, preferred_element_type=jnp.float32
    )
    row_dots = jnp.sum(attn_probs * prob_grads, axis=2, keepdims=True)
    grad_scores = (
        attn_probs * (prob_grads - row_dots) * (1.0 - (capped / softcap) ** 2) * score_scale
    ).astype(jnp.bfloat16)
    grad_query = jnp.einsum(
        "hqk,kd->qhd", grad_scores, key_sel, preferred_element_type=jnp.float32
    )
    grad_key_part = jnp.einsum(
        "hqk,qhd->kd", grad_scores, query_heads, preferred_element_type=jnp.float32
    )
    grad_value_part = jnp.einsum(
        "hqk,qhd->kd",
        attn_probs.astype(jnp.bfloat16),
        out_heads,
        preferred_element_type=jnp.float32,
    )
    cos_all, sin_all = rotary_tables(key_pos, HD)
    grad_key_rot = rotate_back(grad_key_part[:, None, :], cos_all, sin_all).reshape(
        win, kv_width
    )
    kv_grad_win = jnp.concatenate([grad_key_rot, grad_value_part], axis=1).astype(jnp.bfloat16)
    cos_query, sin_query = rotary_tables(query_pos, HD)
    grad_query_round = (
        rotate_back(grad_query, cos_query, sin_query)
        .reshape(quarter_len, part_w)
        .astype(jnp.bfloat16)
    )
    back_rows = 2 * quarter_len + win
    back_all = lax.all_gather(
        jnp.concatenate([attn_out, grad_query_round, kv_grad_win], axis=0),
        ("row", "seq"),
        axis=0,
        tiled=True,
    ).reshape(n_rs, back_rows, part_w)
    out_all = from_blocks(back_all[:, :quarter_len].reshape(n_row, n_seq, quarter_len, part_w))
    grad_query_all = from_blocks(
        back_all[:, quarter_len : 2 * quarter_len].reshape(n_row, n_seq, quarter_len, part_w)
    )
    kv_terms = (
        back_all[:, 2 * quarter_len : 2 * quarter_len + win]
        .astype(jnp.float32)
        .reshape(n_row, n_seq, win, part_w)
        .sum(axis=1)
    )
    kv_grad_f = jnp.zeros((seq_len, part_w), jnp.float32)
    for quarter in range(n_row):
        first = min(max(quarter * quarter_len - doc_back, 0), seq_len - win)
        kv_grad_f = kv_grad_f.at[first : first + win].add(kv_terms[quarter])
    kv_grad_all = kv_grad_f.astype(jnp.bfloat16)

    normed_all = (emb_all_f * inv_all[:, None] * norm_gain[None, :]).astype(jnp.bfloat16)
    grad_wo = jnp.einsum("ln,ld->nd", out_all, grad_all, preferred_element_type=jnp.float32)
    grad_wq = jnp.einsum(
        "ld,ln->dn", normed_all, grad_query_all, preferred_element_type=jnp.float32
    )
    grad_wk = jnp.einsum(
        "ld,ln->dn", normed_all, kv_grad_all[:, :kv_width], preferred_element_type=jnp.float32
    )
    grad_wv = jnp.einsum(
        "ld,ln->dn", normed_all, kv_grad_all[:, kv_width:], preferred_element_type=jnp.float32
    )

    branch_part = jnp.dot(out_all, w_out, preferred_element_type=jnp.float32)
    total_term = jnp.einsum(
        "ln,dn->ld", grad_query_all, w_query, preferred_element_type=jnp.float32
    )
    total_term = total_term + jnp.einsum(
        "ln,dn->ld", kv_grad_all[:, :kv_width], w_key, preferred_element_type=jnp.float32
    )
    total_term = total_term + jnp.einsum(
        "ln,dn->ld", kv_grad_all[:, kv_width:], w_value, preferred_element_type=jnp.float32
    )
    emb_inv_all = emb_all_f * inv_all[:, None]
    gain_terms = jnp.sum(total_term * emb_inv_all, axis=0)
    dot_terms = jnp.sum(total_term * (emb_all_f * norm_gain[None, :]), axis=1)
    col_terms = lax.psum(jnp.concatenate([gain_terms, dot_terms]), "col")
    grad_gain = col_terms[:feat]
    own_dots = lax.dynamic_slice(col_terms[feat:], (col_index * own_len,), (own_len,))
    total_dot = lax.psum(lax.psum(own_dots, "seq"), "row")
    col_sum = lax.psum_scatter(
        jnp.concatenate([branch_part, total_term], axis=1).astype(jnp.bfloat16),
        "col",
        scatter_dimension=0,
        tiled=True,
    ).astype(jnp.float32)
    branch_sum = col_sum[:, :feat]
    grad_normed = col_sum[:, feat:]
    layer_out = (residual + branch_sum).astype(jnp.bfloat16)

    inverse = lax.dynamic_slice(inv_all, (col_index * own_len,), (own_len,))
    scaled_grad = grad_normed * norm_gain[None, :]
    grad_input = (
        out_grad.astype(jnp.float32)
        + inverse[:, None] * scaled_grad
        - residual * (inverse**3 * total_dot / D)[:, None]
    ).astype(jnp.bfloat16)
    return (layer_out, grad_input, grad_gain, grad_wq, grad_wk, grad_wv, grad_wo)


def solution(mesh):
    placed = (
        P("col"),
        P("col"),
        P(),
        P(None, ("row", "seq")),
        P(None, ("row", "seq")),
        P(("row", "seq")),
        P(("row", "seq"), "col"),
        P(("row", "seq"), "col"),
        P(("row", "seq"), "col"),
        P("col", ("row", "seq")),
        P("col", ("row", "seq")),
    )
    return jax.shard_map(
        per_device,
        mesh=mesh,
        in_specs=placed,
        out_specs=(
            P("col", ("row", "seq")),
            P("col", ("row", "seq")),
            P(("row", "seq")),
            P(("row", "seq"), "col"),
            P(("row", "seq"), "col"),
            P(("row", "seq"), "col"),
            P("col", ("row", "seq")),
        ),
        check_vma=False,
    )
```

```python
import jax
import jax.numpy as jnp
from jax import lax
from jax.sharding import PartitionSpec as P
from jax.experimental import pallas as pl

D = 8192
H = 64
KV = 8
HD = 128


epsilon = 1e-05
softcap = 20.0
rope_base = 500000.0
MAX_DOC = 768


def rotary_tables(positions, head_size):
    half_size = head_size // 2
    frequency = rope_base ** (-(jnp.arange(half_size, dtype=jnp.float32) * 2.0) / head_size)
    angles = positions.astype(jnp.float32)[:, None] * frequency[None, :]
    return (jnp.cos(angles), jnp.sin(angles))


def rotate_pairs(values, cosines, sines):
    half_size = values.shape[-1] // 2
    first_half = values[..., :half_size]
    second_half = values[..., half_size:]
    cos_part = cosines[:, None, :]
    sin_part = sines[:, None, :]
    return jnp.concatenate(
        [
            first_half * cos_part - second_half * sin_part,
            second_half * cos_part + first_half * sin_part,
        ],
        axis=-1,
    )


def rotate_back(values, cosines, sines):
    half_size = values.shape[-1] // 2
    first_half = values[..., :half_size]
    second_half = values[..., half_size:]
    cos_part = cosines[:, None, :]
    sin_part = sines[:, None, :]
    return jnp.concatenate(
        [
            first_half * cos_part + second_half * sin_part,
            second_half * cos_part - first_half * sin_part,
        ],
        axis=-1,
    )


def rope_round(values, positions):
    cosines, sines = rotary_tables(positions, HD)
    row_total = values.shape[0]
    return (
        rotate_pairs(values.reshape(row_total, -1, HD), cosines, sines)
        .reshape(row_total, -1)
        .astype(jnp.bfloat16)
    )


def to_blocks(values, n_row, n_seq):
    length, width = values.shape
    return values.reshape(n_row, length // n_row, n_seq, width // n_seq).transpose(0, 2, 1, 3)


def from_blocks(blocks):
    n_row, n_seq, rows, w = blocks.shape
    return blocks.transpose(0, 2, 1, 3).reshape(n_row * rows, n_seq * w)


def project_kernel(lhs_ref, wq_ref, wkv_ref, wo_ref, out_ref):
    feat = wq_ref.shape[0]
    qw = wq_ref.shape[1]
    kw = wkv_ref.shape[1]
    ow = wo_ref.shape[0]
    emb = lhs_ref[:, :feat]
    og = lhs_ref[:, feat:]
    out_ref[:, :qw] = jnp.dot(emb, wq_ref[...], preferred_element_type=jnp.float32)
    out_ref[:, qw : qw + kw] = jnp.dot(emb, wkv_ref[...], preferred_element_type=jnp.float32)
    out_ref[:, qw + kw :] = lax.dot_general(
        og, wo_ref[...], (((1,), (1,)), ((), ())), preferred_element_type=jnp.float32
    )


def project_blocks(lhs, wq, wkv, wo, n_row, n_seq, out_w):
    length, lw = lhs.shape
    feat = wq.shape[0]
    qw = wq.shape[1] // n_seq
    kw = HD
    ow = wo.shape[0] // n_seq
    rows = length // n_row
    flops = 2 * length * feat * (n_seq * (qw + kw + ow))
    return pl.pallas_call(
        project_kernel,
        grid=(n_row, n_seq),
        in_specs=[
            pl.BlockSpec((rows, lw), lambda r, s: (r, 0)),
            pl.BlockSpec((feat, qw), lambda r, s: (0, s)),
            pl.BlockSpec((feat, kw), lambda r, s: (0, s % 2)),
            pl.BlockSpec((ow, feat), lambda r, s: (s, 0)),
        ],
        out_specs=pl.BlockSpec((rows, out_w), lambda r, s: (r * n_seq + s, 0)),
        out_shape=jax.ShapeDtypeStruct((n_row * n_seq * rows, out_w), jnp.float32),
        cost_estimate=pl.CostEstimate(
            flops=flops,
            transcendentals=0,
            bytes_accessed=lhs.size * 2 + (wq.size + wkv.size + wo.size) * 2
            + n_row * n_seq * rows * out_w * 4,
        ),
    )(lhs, wq, wkv, wo)


def per_device(
    motion_ids,
    audio_ids,
    segment_ids,
    motion_table,
    audio_table,
    norm_gain,
    w_query,
    w_key,
    w_value,
    w_out,
    out_grad,
):
    seq_len = segment_ids.shape[0]
    n_row = lax.axis_size("row")
    n_seq = lax.axis_size("seq")
    n_col = lax.axis_size("col")
    row_index = lax.axis_index("row")
    seq_index = lax.axis_index("seq")
    col_index = lax.axis_index("col")
    n_rs = n_row * n_seq
    block_len = seq_len // n_rs
    quarter_len = seq_len // n_row
    own_len = seq_len // n_col
    feat = motion_table.shape[1]
    query_width = w_query.shape[1]
    kv_width = w_key.shape[1]
    head_count = query_width // HD // n_seq
    part_w = head_count * HD
    score_scale = HD ** (-0.5)
    assert kv_width == HD and part_w == 2 * HD

    embedded = (
        jnp.take(motion_table, motion_ids, axis=0).astype(jnp.float32)
        + jnp.take(audio_table, audio_ids, axis=0).astype(jnp.float32)
    ).astype(jnp.bfloat16)
    residual = embedded.astype(jnp.float32)

    both_all = lax.all_gather(
        jnp.concatenate([embedded, out_grad], axis=1), "col", axis=0, tiled=True
    )
    emb_all = both_all[:, :feat]
    grad_all = both_all[:, feat:]
    emb_all_f = emb_all.astype(jnp.float32)
    gain_col = norm_gain[:, None]
    wq_gain = (w_query.astype(jnp.float32) * gain_col).astype(jnp.bfloat16)
    wkv_gain = (
        jnp.concatenate([w_key, w_value], axis=1).astype(jnp.float32) * gain_col
    ).astype(jnp.bfloat16)
    out_w = part_w + HD + part_w
    squares = lax.psum(lax.psum(jnp.sum(emb_all_f * emb_all_f, axis=1), "seq"), "row")
    inv_all = lax.rsqrt(squares / D + epsilon)
    blocks = project_blocks(both_all, wq_gain, wkv_gain, w_out, n_row, n_seq, out_w)
    got = lax.psum_scatter(blocks, ("row", "seq"), scatter_dimension=0, tiled=True)

    q_raw = got[:, :part_w]
    kv_raw = got[:, part_w : part_w + HD]
    d_raw = got[:, part_w + HD : 2 * part_w + HD]
    inv_q = lax.dynamic_slice(inv_all, (row_index * quarter_len,), (quarter_len,))

    query_pos = row_index * quarter_len + jnp.arange(quarter_len, dtype=jnp.int32)
    queries = rope_round(q_raw * inv_q[:, None], query_pos)
    kv_scaled = kv_raw * inv_q[:, None]
    kv_piece = jnp.where(
        seq_index % 2 == 0, rope_round(kv_scaled, query_pos), kv_scaled.astype(jnp.bfloat16)
    )
    out_heads = d_raw.astype(jnp.bfloat16).reshape(quarter_len, head_count, HD)

    kv_gath = lax.all_gather(kv_piece, ("row", "seq"), axis=0, tiled=True).reshape(
        n_row, n_seq, quarter_len, HD
    )
    key_all = kv_gath[:, 0].reshape(seq_len, HD)
    value_all = kv_gath[:, 1].reshape(seq_len, HD)

    doc_back = -(-(MAX_DOC - 1) // quarter_len) * quarter_len
    win = min(seq_len, quarter_len + doc_back)
    win_start = jnp.clip(row_index * quarter_len - doc_back, 0, seq_len - win)
    key_pos = win_start + jnp.arange(win, dtype=jnp.int32)
    key_sel = lax.dynamic_slice(key_all, (win_start, 0), (win, HD))
    value_sel = lax.dynamic_slice(value_all, (win_start, 0), (win, HD))
    key_seg = lax.dynamic_slice(segment_ids, (win_start,), (win,))
    allowed = (key_pos[None, :] <= query_pos[:, None]) & (
        key_seg[None, :] == jnp.take(segment_ids, query_pos)[:, None]
    )
    query_heads = queries.reshape(quarter_len, head_count, HD)
    raw_scores = (
        jnp.einsum("qhd,kd->hqk", query_heads, key_sel, preferred_element_type=jnp.float32)
        * score_scale
    )
    capped = softcap * jnp.tanh(raw_scores / softcap)
    weights = jnp.where(allowed[None], jnp.exp(capped), 0.0)
    totals = jnp.sum(weights, axis=2)
    attended = jnp.einsum(
        "hqk,kd->qhd", weights.astype(jnp.bfloat16), value_sel, preferred_element_type=jnp.float32
    )
    attn_out = (
        (attended / totals.T[:, :, None]).astype(jnp.bfloat16).reshape(quarter_len, part_w)
    )
    attn_probs = weights / totals[:, :, None]
    prob_grads = jnp.einsum(
        "qhd,kd->hqk", out_heads, value_sel, preferred_element_type=jnp.float32
    )
    row_dots = jnp.sum(attn_probs * prob_grads, axis=2, keepdims=True)
    grad_scores = (
        attn_probs * (prob_grads - row_dots) * (1.0 - (capped / softcap) ** 2) * score_scale
    ).astype(jnp.bfloat16)
    grad_query = jnp.einsum(
        "hqk,kd->qhd", grad_scores, key_sel, preferred_element_type=jnp.float32
    )
    grad_key_part = jnp.einsum(
        "hqk,qhd->kd", grad_scores, query_heads, preferred_element_type=jnp.float32
    )
    grad_value_part = jnp.einsum(
        "hqk,qhd->kd",
        attn_probs.astype(jnp.bfloat16),
        out_heads,
        preferred_element_type=jnp.float32,
    )
    cos_all, sin_all = rotary_tables(key_pos, HD)
    grad_key_rot = rotate_back(grad_key_part[:, None, :], cos_all, sin_all).reshape(
        win, kv_width
    )
    kv_grad_win = jnp.concatenate([grad_key_rot, grad_value_part], axis=1).astype(jnp.bfloat16)
    cos_query, sin_query = rotary_tables(query_pos, HD)
    grad_query_round = (
        rotate_back(grad_query, cos_query, sin_query)
        .reshape(quarter_len, part_w)
        .astype(jnp.bfloat16)
    )
    back_rows = 2 * quarter_len + win + 8
    back_all = lax.all_gather(
        jnp.concatenate(
            [attn_out, grad_query_round, kv_grad_win, jnp.zeros((8, part_w), jnp.bfloat16)], axis=0
        ),
        ("row", "seq"),
        axis=0,
        tiled=True,
    ).reshape(n_rs, back_rows, part_w)
    out_all = from_blocks(back_all[:, :quarter_len].reshape(n_row, n_seq, quarter_len, part_w))
    grad_query_all = from_blocks(
        back_all[:, quarter_len : 2 * quarter_len].reshape(n_row, n_seq, quarter_len, part_w)
    )
    kv_terms = (
        back_all[:, 2 * quarter_len : 2 * quarter_len + win]
        .astype(jnp.float32)
        .reshape(n_row, n_seq, win, part_w)
        .sum(axis=1)
    )
    kv_grad_f = jnp.zeros((seq_len, part_w), jnp.float32)
    for quarter in range(n_row):
        first = min(max(quarter * quarter_len - doc_back, 0), seq_len - win)
        kv_grad_f = kv_grad_f.at[first : first + win].add(kv_terms[quarter])
    kv_grad_all = kv_grad_f.astype(jnp.bfloat16)

    normed_all = (emb_all_f * inv_all[:, None] * norm_gain[None, :]).astype(jnp.bfloat16)
    grad_wo = jnp.einsum("ln,ld->nd", out_all, grad_all, preferred_element_type=jnp.float32)
    grad_wq = jnp.einsum(
        "ld,ln->dn", normed_all, grad_query_all, preferred_element_type=jnp.float32
    )
    grad_wk = jnp.einsum(
        "ld,ln->dn", normed_all, kv_grad_all[:, :kv_width], preferred_element_type=jnp.float32
    )
    grad_wv = jnp.einsum(
        "ld,ln->dn", normed_all, kv_grad_all[:, kv_width:], preferred_element_type=jnp.float32
    )

    branch_part = jnp.dot(out_all, w_out, preferred_element_type=jnp.float32)
    total_term = jnp.einsum(
        "ln,dn->ld", grad_query_all, w_query, preferred_element_type=jnp.float32
    )
    total_term = total_term + jnp.einsum(
        "ln,dn->ld", kv_grad_all[:, :kv_width], w_key, preferred_element_type=jnp.float32
    )
    total_term = total_term + jnp.einsum(
        "ln,dn->ld", kv_grad_all[:, kv_width:], w_value, preferred_element_type=jnp.float32
    )
    emb_inv_all = emb_all_f * inv_all[:, None]
    gain_terms = jnp.sum(total_term * emb_inv_all, axis=0)
    dot_terms = jnp.sum(total_term * (emb_all_f * norm_gain[None, :]), axis=1)
    col_terms = lax.psum(jnp.concatenate([gain_terms, dot_terms]), "col")
    grad_gain = col_terms[:feat]
    own_dots = lax.dynamic_slice(col_terms[feat:], (col_index * own_len,), (own_len,))
    total_dot = lax.psum(lax.psum(own_dots, "seq"), "row")
    col_sum = lax.psum_scatter(
        jnp.concatenate([branch_part, total_term], axis=1).astype(jnp.bfloat16),
        "col",
        scatter_dimension=0,
        tiled=True,
    ).astype(jnp.float32)
    branch_sum = col_sum[:, :feat]
    grad_normed = col_sum[:, feat:]
    layer_out = (residual + branch_sum).astype(jnp.bfloat16)

    inverse = lax.dynamic_slice(inv_all, (col_index * own_len,), (own_len,))
    scaled_grad = grad_normed * norm_gain[None, :]
    grad_input = (
        out_grad.astype(jnp.float32)
        + inverse[:, None] * scaled_grad
        - residual * (inverse**3 * total_dot / D)[:, None]
    ).astype(jnp.bfloat16)
    return (layer_out, grad_input, grad_gain, grad_wq, grad_wk, grad_wv, grad_wo)


def solution(mesh):
    placed = (
        P("col"),
        P("col"),
        P(),
        P(None, ("row", "seq")),
        P(None, ("row", "seq")),
        P(("row", "seq")),
        P(("row", "seq"), "col"),
        P(("row", "seq"), "col"),
        P(("row", "seq"), "col"),
        P("col", ("row", "seq")),
        P("col", ("row", "seq")),
    )
    return jax.shard_map(
        per_device,
        mesh=mesh,
        in_specs=placed,
        out_specs=(
            P("col", ("row", "seq")),
            P("col", ("row", "seq")),
            P(("row", "seq")),
            P(("row", "seq"), "col"),
            P(("row", "seq"), "col"),
            P(("row", "seq"), "col"),
            P("col", ("row", "seq")),
        ),
        check_vma=False,
    )
```

```python
import jax
import jax.numpy as jnp
from jax import lax
from jax.sharding import PartitionSpec as P
from jax.experimental import pallas as pl
from jax.experimental.pallas import tpu as pltpu

D = 8192
H = 64
KV = 8
HD = 128


epsilon = 1e-05
softcap = 20.0
rope_base = 500000.0
MAX_DOC = 768


def rotary_tables(positions, head_size):
    half_size = head_size // 2
    frequency = rope_base ** (-(jnp.arange(half_size, dtype=jnp.float32) * 2.0) / head_size)
    angles = positions.astype(jnp.float32)[:, None] * frequency[None, :]
    return (jnp.cos(angles), jnp.sin(angles))


def rotate_pairs(values, cosines, sines):
    half_size = values.shape[-1] // 2
    first_half = values[..., :half_size]
    second_half = values[..., half_size:]
    cos_part = cosines[:, None, :]
    sin_part = sines[:, None, :]
    return jnp.concatenate(
        [
            first_half * cos_part - second_half * sin_part,
            second_half * cos_part + first_half * sin_part,
        ],
        axis=-1,
    )


def rotate_back(values, cosines, sines):
    half_size = values.shape[-1] // 2
    first_half = values[..., :half_size]
    second_half = values[..., half_size:]
    cos_part = cosines[:, None, :]
    sin_part = sines[:, None, :]
    return jnp.concatenate(
        [
            first_half * cos_part + second_half * sin_part,
            second_half * cos_part - first_half * sin_part,
        ],
        axis=-1,
    )


def rope_round(values, positions):
    cosines, sines = rotary_tables(positions, HD)
    row_total = values.shape[0]
    return (
        rotate_pairs(values.reshape(row_total, -1, HD), cosines, sines)
        .reshape(row_total, -1)
        .astype(jnp.bfloat16)
    )


def to_blocks(values, n_row, n_seq):
    length, width = values.shape
    return values.reshape(n_row, length // n_row, n_seq, width // n_seq).transpose(0, 2, 1, 3)


def from_blocks(blocks):
    n_row, n_seq, rows, w = blocks.shape
    return blocks.transpose(0, 2, 1, 3).reshape(n_row * rows, n_seq * w)


def project_kernel(lhs_ref, wq_ref, wkv_ref, wo_ref, out_ref):
    feat = wq_ref.shape[0]
    qw = wq_ref.shape[1]
    kw = wkv_ref.shape[1]
    ow = wo_ref.shape[0]
    emb = lhs_ref[:, :feat]
    og = lhs_ref[:, feat:]
    out_ref[:, :qw] = jnp.dot(emb, wq_ref[...], preferred_element_type=jnp.float32)
    out_ref[:, qw : qw + kw] = jnp.dot(emb, wkv_ref[...], preferred_element_type=jnp.float32)
    out_ref[:, qw + kw :] = lax.dot_general(
        og, wo_ref[...], (((1,), (1,)), ((), ())), preferred_element_type=jnp.float32
    )


def project_blocks(lhs, wq, wkv, wo, n_row, n_seq, out_w):
    length, lw = lhs.shape
    feat = wq.shape[0]
    qw = wq.shape[1] // n_seq
    kw = HD
    ow = wo.shape[0] // n_seq
    rows = length // n_row
    flops = 2 * length * feat * (n_seq * (qw + kw + ow))
    return pl.pallas_call(
        project_kernel,
        grid=(n_row, n_seq),
        in_specs=[
            pl.BlockSpec((rows, lw), lambda r, s: (r, 0)),
            pl.BlockSpec((feat, qw), lambda r, s: (0, s)),
            pl.BlockSpec((feat, kw), lambda r, s: (0, s % 2)),
            pl.BlockSpec((ow, feat), lambda r, s: (s, 0)),
        ],
        out_specs=pl.BlockSpec((rows, out_w), lambda r, s: (r * n_seq + s, 0)),
        out_shape=jax.ShapeDtypeStruct((n_row * n_seq * rows, out_w), jnp.float32),
        cost_estimate=pl.CostEstimate(
            flops=flops,
            transcendentals=0,
            bytes_accessed=lhs.size * 2 + (wq.size + wkv.size + wo.size) * 2
            + n_row * n_seq * rows * out_w * 4,
        ),
    )(lhs, wq, wkv, wo)


def attention_kernel(
    q_ref, do_ref, k_ref, v_ref, qpos_ref, qseg_ref, kpos_ref, kseg_ref,
    out_ref, gq_ref, gk_ref, gv_ref,
):
    head = pl.program_id(0)
    score_scale = HD ** (-0.5)
    query = q_ref[0]
    dout = do_ref[0]
    key = k_ref[...]
    value = v_ref[...]
    allowed = (kpos_ref[...] <= qpos_ref[...]) & (kseg_ref[...] == qseg_ref[...])
    nt = (((1,), (1,)), ((), ()))
    tn = (((0,), (0,)), ((), ()))
    raw_scores = (
        lax.dot_general(query, key, nt, preferred_element_type=jnp.float32) * score_scale
    )
    capped = softcap * jnp.tanh(raw_scores / softcap)
    weights = jnp.where(allowed, jnp.exp(capped), 0.0)
    totals = jnp.sum(weights, axis=1, keepdims=True)
    attended = jnp.dot(
        weights.astype(jnp.bfloat16), value, preferred_element_type=jnp.float32
    )
    out_ref[0] = (attended / totals).astype(out_ref.dtype)
    probs = weights / totals
    prob_grads = lax.dot_general(dout, value, nt, preferred_element_type=jnp.float32)
    row_dots = jnp.sum(probs * prob_grads, axis=1, keepdims=True)
    grad_scores = (
        probs * (prob_grads - row_dots) * (1.0 - (capped / softcap) ** 2) * score_scale
    ).astype(jnp.bfloat16)
    gq_ref[0] = jnp.dot(grad_scores, key, preferred_element_type=jnp.float32)
    gk_term = lax.dot_general(grad_scores, query, tn, preferred_element_type=jnp.float32)
    gv_term = lax.dot_general(
        probs.astype(jnp.bfloat16), dout, tn, preferred_element_type=jnp.float32
    )

    @pl.when(head == 0)
    def _():
        gk_ref[...] = gk_term
        gv_ref[...] = gv_term

    @pl.when(head != 0)
    def _():
        gk_ref[...] += gk_term
        gv_ref[...] += gv_term


def attention_block(q, dout, key, value, qpos, qseg, kpos, kseg):
    heads, rows, hd = q.shape
    win = key.shape[0]
    full = lambda h: (0, 0)
    per_head = lambda h: (h, 0, 0)
    return pl.pallas_call(
        attention_kernel,
        grid=(heads,),
        in_specs=[
            pl.BlockSpec((1, rows, hd), per_head),
            pl.BlockSpec((1, rows, hd), per_head),
            pl.BlockSpec((win, hd), full),
            pl.BlockSpec((win, hd), full),
            pl.BlockSpec((rows, 1), full),
            pl.BlockSpec((rows, 1), full),
            pl.BlockSpec((1, win), full),
            pl.BlockSpec((1, win), full),
        ],
        out_specs=[
            pl.BlockSpec((1, rows, hd), per_head),
            pl.BlockSpec((1, rows, hd), per_head),
            pl.BlockSpec((win, hd), full),
            pl.BlockSpec((win, hd), full),
        ],
        out_shape=[
            jax.ShapeDtypeStruct((heads, rows, hd), jnp.bfloat16),
            jax.ShapeDtypeStruct((heads, rows, hd), jnp.float32),
            jax.ShapeDtypeStruct((win, hd), jnp.float32),
            jax.ShapeDtypeStruct((win, hd), jnp.float32),
        ],
        compiler_params=pltpu.CompilerParams(
            dimension_semantics=("arbitrary",), vmem_limit_bytes=48 * 1024 * 1024
        ),
        cost_estimate=pl.CostEstimate(
            flops=12 * heads * rows * win * hd,
            transcendentals=2 * heads * rows * win,
            bytes_accessed=4 * heads * rows * hd * 2 + 4 * win * hd * 4,
        ),
    )(q, dout, key, value, qpos, qseg, kpos, kseg)


def per_device(
    motion_ids,
    audio_ids,
    segment_ids,
    motion_table,
    audio_table,
    norm_gain,
    w_query,
    w_key,
    w_value,
    w_out,
    out_grad,
):
    seq_len = segment_ids.shape[0]
    n_row = lax.axis_size("row")
    n_seq = lax.axis_size("seq")
    n_col = lax.axis_size("col")
    row_index = lax.axis_index("row")
    seq_index = lax.axis_index("seq")
    col_index = lax.axis_index("col")
    n_rs = n_row * n_seq
    block_len = seq_len // n_rs
    quarter_len = seq_len // n_row
    own_len = seq_len // n_col
    feat = motion_table.shape[1]
    query_width = w_query.shape[1]
    kv_width = w_key.shape[1]
    head_count = query_width // HD // n_seq
    part_w = head_count * HD
    score_scale = HD ** (-0.5)
    assert kv_width == HD and part_w == 2 * HD

    embedded = (
        jnp.take(motion_table, motion_ids, axis=0).astype(jnp.float32)
        + jnp.take(audio_table, audio_ids, axis=0).astype(jnp.float32)
    ).astype(jnp.bfloat16)
    residual = embedded.astype(jnp.float32)

    both_all = lax.all_gather(
        jnp.concatenate([embedded, out_grad], axis=1), "col", axis=0, tiled=True
    )
    emb_all = both_all[:, :feat]
    grad_all = both_all[:, feat:]
    emb_all_f = emb_all.astype(jnp.float32)
    gain_col = norm_gain[:, None]
    wq_gain = (w_query.astype(jnp.float32) * gain_col).astype(jnp.bfloat16)
    wkv_gain = (
        jnp.concatenate([w_key, w_value], axis=1).astype(jnp.float32) * gain_col
    ).astype(jnp.bfloat16)
    out_w = part_w + HD + part_w
    squares = lax.psum(lax.psum(jnp.sum(emb_all_f * emb_all_f, axis=1), "seq"), "row")
    inv_all = lax.rsqrt(squares / D + epsilon)
    blocks = project_blocks(both_all, wq_gain, wkv_gain, w_out, n_row, n_seq, out_w)
    got = lax.psum_scatter(blocks, ("row", "seq"), scatter_dimension=0, tiled=True)

    q_raw = got[:, :part_w]
    kv_raw = got[:, part_w : part_w + HD]
    d_raw = got[:, part_w + HD : 2 * part_w + HD]
    inv_q = lax.dynamic_slice(inv_all, (row_index * quarter_len,), (quarter_len,))

    query_pos = row_index * quarter_len + jnp.arange(quarter_len, dtype=jnp.int32)
    queries = rope_round(q_raw * inv_q[:, None], query_pos)
    kv_scaled = kv_raw * inv_q[:, None]
    kv_piece = jnp.where(
        seq_index % 2 == 0, rope_round(kv_scaled, query_pos), kv_scaled.astype(jnp.bfloat16)
    )
    out_heads = d_raw.astype(jnp.bfloat16).reshape(quarter_len, head_count, HD)

    kv_gath = lax.all_gather(kv_piece, ("row", "seq"), axis=0, tiled=True).reshape(
        n_row, n_seq, quarter_len, HD
    )
    key_all = kv_gath[:, 0].reshape(seq_len, HD)
    value_all = kv_gath[:, 1].reshape(seq_len, HD)

    doc_back = -(-(MAX_DOC - 1) // quarter_len) * quarter_len
    win = min(seq_len, quarter_len + doc_back)
    win_start = jnp.clip(row_index * quarter_len - doc_back, 0, seq_len - win)
    key_pos = win_start + jnp.arange(win, dtype=jnp.int32)
    key_sel = lax.dynamic_slice(key_all, (win_start, 0), (win, HD))
    value_sel = lax.dynamic_slice(value_all, (win_start, 0), (win, HD))
    key_seg = lax.dynamic_slice(segment_ids, (win_start,), (win,))
    query_seg = jnp.take(segment_ids, query_pos)
    attn_heads, grad_query_heads, grad_key_part, grad_value_part = attention_block(
        queries.reshape(quarter_len, head_count, HD).transpose(1, 0, 2),
        out_heads.transpose(1, 0, 2),
        key_sel,
        value_sel,
        query_pos[:, None],
        query_seg[:, None],
        key_pos[None, :],
        key_seg[None, :],
    )
    attn_out = attn_heads.transpose(1, 0, 2).reshape(quarter_len, part_w)
    grad_query = grad_query_heads.transpose(1, 0, 2)
    cos_all, sin_all = rotary_tables(key_pos, HD)
    grad_key_rot = rotate_back(grad_key_part[:, None, :], cos_all, sin_all).reshape(
        win, kv_width
    )
    kv_grad_win = jnp.concatenate([grad_key_rot, grad_value_part], axis=1).astype(jnp.bfloat16)
    cos_query, sin_query = rotary_tables(query_pos, HD)
    grad_query_round = (
        rotate_back(grad_query, cos_query, sin_query)
        .reshape(quarter_len, part_w)
        .astype(jnp.bfloat16)
    )
    back_rows = 2 * quarter_len + win + 8
    back_all = lax.all_gather(
        jnp.concatenate(
            [attn_out, grad_query_round, kv_grad_win, jnp.zeros((8, part_w), jnp.bfloat16)], axis=0
        ),
        ("row", "seq"),
        axis=0,
        tiled=True,
    ).reshape(n_rs, back_rows, part_w)
    out_all = from_blocks(back_all[:, :quarter_len].reshape(n_row, n_seq, quarter_len, part_w))
    grad_query_all = from_blocks(
        back_all[:, quarter_len : 2 * quarter_len].reshape(n_row, n_seq, quarter_len, part_w)
    )
    kv_terms = (
        back_all[:, 2 * quarter_len : 2 * quarter_len + win]
        .astype(jnp.float32)
        .reshape(n_row, n_seq, win, part_w)
        .sum(axis=1)
    )
    kv_grad_f = jnp.zeros((seq_len, part_w), jnp.float32)
    for quarter in range(n_row):
        first = min(max(quarter * quarter_len - doc_back, 0), seq_len - win)
        kv_grad_f = kv_grad_f.at[first : first + win].add(kv_terms[quarter])
    kv_grad_all = kv_grad_f.astype(jnp.bfloat16)

    normed_all = (emb_all_f * inv_all[:, None] * norm_gain[None, :]).astype(jnp.bfloat16)
    grad_wo = jnp.einsum("ln,ld->nd", out_all, grad_all, preferred_element_type=jnp.float32)
    grad_wq = jnp.einsum(
        "ld,ln->dn", normed_all, grad_query_all, preferred_element_type=jnp.float32
    )
    grad_wk = jnp.einsum(
        "ld,ln->dn", normed_all, kv_grad_all[:, :kv_width], preferred_element_type=jnp.float32
    )
    grad_wv = jnp.einsum(
        "ld,ln->dn", normed_all, kv_grad_all[:, kv_width:], preferred_element_type=jnp.float32
    )

    branch_part = jnp.dot(out_all, w_out, preferred_element_type=jnp.float32)
    total_term = jnp.einsum(
        "ln,dn->ld", grad_query_all, w_query, preferred_element_type=jnp.float32
    )
    total_term = total_term + jnp.einsum(
        "ln,dn->ld", kv_grad_all[:, :kv_width], w_key, preferred_element_type=jnp.float32
    )
    total_term = total_term + jnp.einsum(
        "ln,dn->ld", kv_grad_all[:, kv_width:], w_value, preferred_element_type=jnp.float32
    )
    emb_inv_all = emb_all_f * inv_all[:, None]
    gain_terms = jnp.sum(total_term * emb_inv_all, axis=0)
    dot_terms = jnp.sum(total_term * (emb_all_f * norm_gain[None, :]), axis=1)
    col_terms = lax.psum(jnp.concatenate([gain_terms, dot_terms]), "col")
    grad_gain = col_terms[:feat]
    own_dots = lax.dynamic_slice(col_terms[feat:], (col_index * own_len,), (own_len,))
    total_dot = lax.psum(lax.psum(own_dots, "seq"), "row")
    col_sum = lax.psum_scatter(
        jnp.concatenate([branch_part, total_term], axis=1).astype(jnp.bfloat16),
        "col",
        scatter_dimension=0,
        tiled=True,
    ).astype(jnp.float32)
    branch_sum = col_sum[:, :feat]
    grad_normed = col_sum[:, feat:]
    layer_out = (residual + branch_sum).astype(jnp.bfloat16)

    inverse = lax.dynamic_slice(inv_all, (col_index * own_len,), (own_len,))
    scaled_grad = grad_normed * norm_gain[None, :]
    grad_input = (
        out_grad.astype(jnp.float32)
        + inverse[:, None] * scaled_grad
        - residual * (inverse**3 * total_dot / D)[:, None]
    ).astype(jnp.bfloat16)
    return (layer_out, grad_input, grad_gain, grad_wq, grad_wk, grad_wv, grad_wo)


def solution(mesh):
    placed = (
        P("col"),
        P("col"),
        P(),
        P(None, ("row", "seq")),
        P(None, ("row", "seq")),
        P(("row", "seq")),
        P(("row", "seq"), "col"),
        P(("row", "seq"), "col"),
        P(("row", "seq"), "col"),
        P("col", ("row", "seq")),
        P("col", ("row", "seq")),
    )
    return jax.shard_map(
        per_device,
        mesh=mesh,
        in_specs=placed,
        out_specs=(
            P("col", ("row", "seq")),
            P("col", ("row", "seq")),
            P(("row", "seq")),
            P(("row", "seq"), "col"),
            P(("row", "seq"), "col"),
            P(("row", "seq"), "col"),
            P("col", ("row", "seq")),
        ),
        check_vma=False,
    )
```

```python
import jax
import jax.numpy as jnp
from jax import lax
from jax.sharding import PartitionSpec as P
from jax.experimental import pallas as pl
from jax.experimental.pallas import tpu as pltpu

D = 8192
H = 64
KV = 8
HD = 128


epsilon = 1e-05
softcap = 20.0
rope_base = 500000.0
MAX_DOC = 768


def rotary_tables(positions, head_size):
    half_size = head_size // 2
    frequency = rope_base ** (-(jnp.arange(half_size, dtype=jnp.float32) * 2.0) / head_size)
    angles = positions.astype(jnp.float32)[:, None] * frequency[None, :]
    return (jnp.cos(angles), jnp.sin(angles))


def rotate_pairs(values, cosines, sines):
    half_size = values.shape[-1] // 2
    first_half = values[..., :half_size]
    second_half = values[..., half_size:]
    cos_part = cosines[:, None, :]
    sin_part = sines[:, None, :]
    return jnp.concatenate(
        [
            first_half * cos_part - second_half * sin_part,
            second_half * cos_part + first_half * sin_part,
        ],
        axis=-1,
    )


def rotate_back(values, cosines, sines):
    half_size = values.shape[-1] // 2
    first_half = values[..., :half_size]
    second_half = values[..., half_size:]
    cos_part = cosines[:, None, :]
    sin_part = sines[:, None, :]
    return jnp.concatenate(
        [
            first_half * cos_part + second_half * sin_part,
            second_half * cos_part - first_half * sin_part,
        ],
        axis=-1,
    )


def rope_round(values, positions):
    cosines, sines = rotary_tables(positions, HD)
    row_total = values.shape[0]
    return (
        rotate_pairs(values.reshape(row_total, -1, HD), cosines, sines)
        .reshape(row_total, -1)
        .astype(jnp.bfloat16)
    )


def to_blocks(values, n_row, n_seq):
    length, width = values.shape
    return values.reshape(n_row, length // n_row, n_seq, width // n_seq).transpose(0, 2, 1, 3)


def from_blocks(blocks):
    n_row, n_seq, rows, w = blocks.shape
    return blocks.transpose(0, 2, 1, 3).reshape(n_row * rows, n_seq * w)


def project_kernel(lhs_ref, wq_ref, wkv_ref, wo_ref, out_ref):
    feat = wq_ref.shape[0]
    qw = wq_ref.shape[1]
    kw = wkv_ref.shape[1]
    ow = wo_ref.shape[0]
    emb = lhs_ref[:, :feat]
    og = lhs_ref[:, feat:]
    out_ref[:, :qw] = jnp.dot(emb, wq_ref[...], preferred_element_type=jnp.float32)
    out_ref[:, qw : qw + kw] = jnp.dot(emb, wkv_ref[...], preferred_element_type=jnp.float32)
    out_ref[:, qw + kw :] = lax.dot_general(
        og, wo_ref[...], (((1,), (1,)), ((), ())), preferred_element_type=jnp.float32
    )


def project_blocks(lhs, wq, wkv, wo, n_row, n_seq, out_w):
    length, lw = lhs.shape
    feat = wq.shape[0]
    qw = wq.shape[1] // n_seq
    kw = HD
    ow = wo.shape[0] // n_seq
    rows = length // n_row
    flops = 2 * length * feat * (n_seq * (qw + kw + ow))
    return pl.pallas_call(
        project_kernel,
        grid=(n_row, n_seq),
        in_specs=[
            pl.BlockSpec((rows, lw), lambda r, s: (r, 0)),
            pl.BlockSpec((feat, qw), lambda r, s: (0, s)),
            pl.BlockSpec((feat, kw), lambda r, s: (0, s % 2)),
            pl.BlockSpec((ow, feat), lambda r, s: (s, 0)),
        ],
        out_specs=pl.BlockSpec((rows, out_w), lambda r, s: (r * n_seq + s, 0)),
        out_shape=jax.ShapeDtypeStruct((n_row * n_seq * rows, out_w), jnp.float32),
        cost_estimate=pl.CostEstimate(
            flops=flops,
            transcendentals=0,
            bytes_accessed=lhs.size * 2 + (wq.size + wkv.size + wo.size) * 2
            + n_row * n_seq * rows * out_w * 4,
        ),
    )(lhs, wq, wkv, wo)


def attention_kernel(
    q_ref, do_ref, k_ref, v_ref, qpos_ref, qseg_ref, kpos_ref, kseg_ref,
    out_ref, gq_ref, gk_ref, gv_ref,
):
    head = pl.program_id(0)
    score_scale = HD ** (-0.5)
    query = q_ref[0]
    dout = do_ref[0]
    key = k_ref[...]
    value = v_ref[...]
    allowed = (kpos_ref[...] <= qpos_ref[...]) & (kseg_ref[...] == qseg_ref[...])
    nt = (((1,), (1,)), ((), ()))
    tn = (((0,), (0,)), ((), ()))
    raw_scores = (
        lax.dot_general(query, key, nt, preferred_element_type=jnp.float32) * score_scale
    )
    capped = softcap * jnp.tanh(raw_scores / softcap)
    weights = jnp.where(allowed, jnp.exp(capped), 0.0)
    totals = jnp.sum(weights, axis=1, keepdims=True)
    attended = jnp.dot(
        weights.astype(jnp.bfloat16), value, preferred_element_type=jnp.float32
    )
    out_ref[0] = (attended / totals).astype(out_ref.dtype)
    probs = weights / totals
    prob_grads = lax.dot_general(dout, value, nt, preferred_element_type=jnp.float32)
    row_dots = jnp.sum(probs * prob_grads, axis=1, keepdims=True)
    grad_scores = (
        probs * (prob_grads - row_dots) * (1.0 - (capped / softcap) ** 2) * score_scale
    ).astype(jnp.bfloat16)
    gq_ref[0] = jnp.dot(grad_scores, key, preferred_element_type=jnp.float32)
    gk_term = lax.dot_general(grad_scores, query, tn, preferred_element_type=jnp.float32)
    gv_term = lax.dot_general(
        probs.astype(jnp.bfloat16), dout, tn, preferred_element_type=jnp.float32
    )

    @pl.when(head == 0)
    def _():
        gk_ref[...] = gk_term
        gv_ref[...] = gv_term

    @pl.when(head != 0)
    def _():
        gk_ref[...] += gk_term
        gv_ref[...] += gv_term


def attention_block(q, dout, key, value, qpos, qseg, kpos, kseg):
    heads, rows, hd = q.shape
    win = key.shape[0]
    full = lambda h: (0, 0)
    per_head = lambda h: (h, 0, 0)
    return pl.pallas_call(
        attention_kernel,
        grid=(heads,),
        in_specs=[
            pl.BlockSpec((1, rows, hd), per_head),
            pl.BlockSpec((1, rows, hd), per_head),
            pl.BlockSpec((win, hd), full),
            pl.BlockSpec((win, hd), full),
            pl.BlockSpec((rows, 1), full),
            pl.BlockSpec((rows, 1), full),
            pl.BlockSpec((1, win), full),
            pl.BlockSpec((1, win), full),
        ],
        out_specs=[
            pl.BlockSpec((1, rows, hd), per_head),
            pl.BlockSpec((1, rows, hd), per_head),
            pl.BlockSpec((win, hd), full),
            pl.BlockSpec((win, hd), full),
        ],
        out_shape=[
            jax.ShapeDtypeStruct((heads, rows, hd), jnp.bfloat16),
            jax.ShapeDtypeStruct((heads, rows, hd), jnp.float32),
            jax.ShapeDtypeStruct((win, hd), jnp.float32),
            jax.ShapeDtypeStruct((win, hd), jnp.float32),
        ],
        compiler_params=pltpu.CompilerParams(
            dimension_semantics=("arbitrary",), vmem_limit_bytes=48 * 1024 * 1024
        ),
        cost_estimate=pl.CostEstimate(
            flops=12 * heads * rows * win * hd,
            transcendentals=2 * heads * rows * win,
            bytes_accessed=4 * heads * rows * hd * 2 + 4 * win * hd * 4,
        ),
    )(q, dout, key, value, qpos, qseg, kpos, kseg)


def per_device(
    motion_ids,
    audio_ids,
    segment_ids,
    motion_table,
    audio_table,
    norm_gain,
    w_query,
    w_key,
    w_value,
    w_out,
    out_grad,
):
    seq_len = segment_ids.shape[0]
    n_row = lax.axis_size("row")
    n_seq = lax.axis_size("seq")
    n_col = lax.axis_size("col")
    row_index = lax.axis_index("row")
    seq_index = lax.axis_index("seq")
    col_index = lax.axis_index("col")
    n_rs = n_row * n_seq
    block_len = seq_len // n_rs
    quarter_len = seq_len // n_row
    own_len = seq_len // n_col
    feat = motion_table.shape[1]
    query_width = w_query.shape[1]
    kv_width = w_key.shape[1]
    head_count = query_width // HD // n_seq
    part_w = head_count * HD
    score_scale = HD ** (-0.5)
    assert kv_width == HD and part_w == 2 * HD

    embedded = (
        jnp.take(motion_table, motion_ids, axis=0).astype(jnp.float32)
        + jnp.take(audio_table, audio_ids, axis=0).astype(jnp.float32)
    ).astype(jnp.bfloat16)
    residual = embedded.astype(jnp.float32)

    both_all = lax.all_gather(
        jnp.concatenate([embedded, out_grad], axis=1), "col", axis=0, tiled=True
    )
    emb_all = both_all[:, :feat]
    grad_all = both_all[:, feat:]
    emb_all_f = emb_all.astype(jnp.float32)
    gain_col = norm_gain[:, None]
    wq_gain = (w_query.astype(jnp.float32) * gain_col).astype(jnp.bfloat16)
    wkv_gain = (
        jnp.concatenate([w_key, w_value], axis=1).astype(jnp.float32) * gain_col
    ).astype(jnp.bfloat16)
    out_w = part_w + HD + part_w
    squares = lax.psum(lax.psum(jnp.sum(emb_all_f * emb_all_f, axis=1), "seq"), "row")
    inv_all = lax.rsqrt(squares / D + epsilon)
    blocks = project_blocks(both_all, wq_gain, wkv_gain, w_out, n_row, n_seq, out_w)
    got = lax.psum_scatter(blocks, ("row", "seq"), scatter_dimension=0, tiled=True)

    q_raw = got[:, :part_w]
    kv_raw = got[:, part_w : part_w + HD]
    d_raw = got[:, part_w + HD : 2 * part_w + HD]
    inv_q = lax.dynamic_slice(inv_all, (row_index * quarter_len,), (quarter_len,))

    query_pos = row_index * quarter_len + jnp.arange(quarter_len, dtype=jnp.int32)
    queries = rope_round(q_raw * inv_q[:, None], query_pos)
    kv_scaled = kv_raw * inv_q[:, None]
    kv_piece = jnp.where(
        seq_index % 2 == 0, rope_round(kv_scaled, query_pos), kv_scaled.astype(jnp.bfloat16)
    )
    out_heads = d_raw.astype(jnp.bfloat16).reshape(quarter_len, head_count, HD)

    kv_gath = lax.all_gather(kv_piece, ("row", "seq"), axis=0, tiled=True).reshape(
        n_row, n_seq, quarter_len, HD
    )
    key_all = kv_gath[:, 0].reshape(seq_len, HD)
    value_all = kv_gath[:, 1].reshape(seq_len, HD)

    doc_back = -(-(MAX_DOC - 1) // quarter_len) * quarter_len
    win = min(seq_len, quarter_len + doc_back)
    win_start = jnp.clip(row_index * quarter_len - doc_back, 0, seq_len - win)
    key_pos = win_start + jnp.arange(win, dtype=jnp.int32)
    key_sel = lax.dynamic_slice(key_all, (win_start, 0), (win, HD))
    value_sel = lax.dynamic_slice(value_all, (win_start, 0), (win, HD))
    key_seg = lax.dynamic_slice(segment_ids, (win_start,), (win,))
    query_seg = jnp.take(segment_ids, query_pos)
    attn_heads, grad_query_heads, grad_key_part, grad_value_part = attention_block(
        queries.reshape(quarter_len, head_count, HD).transpose(1, 0, 2),
        out_heads.transpose(1, 0, 2),
        key_sel,
        value_sel,
        query_pos[:, None],
        query_seg[:, None],
        key_pos[None, :],
        key_seg[None, :],
    )
    attn_out = attn_heads.transpose(1, 0, 2).reshape(quarter_len, part_w)
    grad_query = grad_query_heads.transpose(1, 0, 2)
    cos_all, sin_all = rotary_tables(key_pos, HD)
    grad_key_rot = rotate_back(grad_key_part[:, None, :], cos_all, sin_all).reshape(
        win, kv_width
    )
    kv_grad_win = jnp.concatenate([grad_key_rot, grad_value_part], axis=1).astype(jnp.bfloat16)
    cos_query, sin_query = rotary_tables(query_pos, HD)
    grad_query_round = (
        rotate_back(grad_query, cos_query, sin_query)
        .reshape(quarter_len, part_w)
        .astype(jnp.bfloat16)
    )
    back_rows = 2 * quarter_len + win + 8
    back_all = lax.all_gather(
        jnp.concatenate(
            [attn_out, grad_query_round, kv_grad_win, jnp.zeros((8, part_w), jnp.bfloat16)], axis=0
        ),
        ("row", "seq"),
        axis=0,
        tiled=True,
    ).reshape(n_rs, back_rows, part_w)
    out_blk = back_all[:, :quarter_len].reshape(n_row, n_seq, quarter_len, part_w)
    gq_blk = back_all[:, quarter_len : 2 * quarter_len].reshape(n_row, n_seq, quarter_len, part_w)
    kv_terms = (
        back_all[:, 2 * quarter_len : 2 * quarter_len + win]
        .astype(jnp.float32)
        .reshape(n_row, n_seq, win, part_w)
        .sum(axis=1)
    )
    kv_grad_f = jnp.zeros((seq_len, part_w), jnp.float32)
    for quarter in range(n_row):
        first = min(max(quarter * quarter_len - doc_back, 0), seq_len - win)
        kv_grad_f = kv_grad_f.at[first : first + win].add(kv_terms[quarter])
    kv_grad_all = kv_grad_f.astype(jnp.bfloat16)

    normed_all = (emb_all_f * inv_all[:, None] * norm_gain[None, :]).astype(jnp.bfloat16)
    grad_wo = jnp.einsum(
        "rspn,rpd->snd",
        out_blk,
        grad_all.reshape(n_row, quarter_len, feat),
        preferred_element_type=jnp.float32,
    ).reshape(query_width, feat)
    grad_wq = jnp.einsum(
        "rpd,rspn->dsn",
        normed_all.reshape(n_row, quarter_len, feat),
        gq_blk,
        preferred_element_type=jnp.float32,
    ).reshape(feat, query_width)
    grad_wk = jnp.einsum(
        "ld,ln->dn", normed_all, kv_grad_all[:, :kv_width], preferred_element_type=jnp.float32
    )
    grad_wv = jnp.einsum(
        "ld,ln->dn", normed_all, kv_grad_all[:, kv_width:], preferred_element_type=jnp.float32
    )

    branch_part = jnp.einsum(
        "rspn,snd->rpd",
        out_blk,
        w_out.reshape(n_seq, part_w, feat),
        preferred_element_type=jnp.float32,
    ).reshape(seq_len, feat)
    total_term = jnp.einsum(
        "rspn,dsn->rpd",
        gq_blk,
        w_query.reshape(feat, n_seq, part_w),
        preferred_element_type=jnp.float32,
    ).reshape(seq_len, feat)
    total_term = total_term + jnp.einsum(
        "ln,dn->ld", kv_grad_all[:, :kv_width], w_key, preferred_element_type=jnp.float32
    )
    total_term = total_term + jnp.einsum(
        "ln,dn->ld", kv_grad_all[:, kv_width:], w_value, preferred_element_type=jnp.float32
    )
    emb_inv_all = emb_all_f * inv_all[:, None]
    gain_terms = jnp.sum(total_term * emb_inv_all, axis=0)
    dot_terms = jnp.sum(total_term * (emb_all_f * norm_gain[None, :]), axis=1)
    col_terms = lax.psum(jnp.concatenate([gain_terms, dot_terms]), "col")
    grad_gain = col_terms[:feat]
    own_dots = lax.dynamic_slice(col_terms[feat:], (col_index * own_len,), (own_len,))
    total_dot = lax.psum(lax.psum(own_dots, "seq"), "row")
    col_sum = lax.psum_scatter(
        jnp.concatenate([branch_part, total_term], axis=1).astype(jnp.bfloat16),
        "col",
        scatter_dimension=0,
        tiled=True,
    ).astype(jnp.float32)
    branch_sum = col_sum[:, :feat]
    grad_normed = col_sum[:, feat:]
    layer_out = (residual + branch_sum).astype(jnp.bfloat16)

    inverse = lax.dynamic_slice(inv_all, (col_index * own_len,), (own_len,))
    scaled_grad = grad_normed * norm_gain[None, :]
    grad_input = (
        out_grad.astype(jnp.float32)
        + inverse[:, None] * scaled_grad
        - residual * (inverse**3 * total_dot / D)[:, None]
    ).astype(jnp.bfloat16)
    return (layer_out, grad_input, grad_gain, grad_wq, grad_wk, grad_wv, grad_wo)


def solution(mesh):
    placed = (
        P("col"),
        P("col"),
        P(),
        P(None, ("row", "seq")),
        P(None, ("row", "seq")),
        P(("row", "seq")),
        P(("row", "seq"), "col"),
        P(("row", "seq"), "col"),
        P(("row", "seq"), "col"),
        P("col", ("row", "seq")),
        P("col", ("row", "seq")),
    )
    return jax.shard_map(
        per_device,
        mesh=mesh,
        in_specs=placed,
        out_specs=(
            P("col", ("row", "seq")),
            P("col", ("row", "seq")),
            P(("row", "seq")),
            P(("row", "seq"), "col"),
            P(("row", "seq"), "col"),
            P(("row", "seq"), "col"),
            P("col", ("row", "seq")),
        ),
        check_vma=False,
    )
```

```python
import jax
import jax.numpy as jnp
from jax import lax
from jax.sharding import PartitionSpec as P
from jax.experimental import pallas as pl
from jax.experimental.pallas import tpu as pltpu

D = 8192
H = 64
KV = 8
HD = 128


epsilon = 1e-05
softcap = 20.0
rope_base = 500000.0
MAX_DOC = 768


def rotary_tables(positions, head_size):
    half_size = head_size // 2
    frequency = rope_base ** (-(jnp.arange(half_size, dtype=jnp.float32) * 2.0) / head_size)
    angles = positions.astype(jnp.float32)[:, None] * frequency[None, :]
    return (jnp.cos(angles), jnp.sin(angles))


def rotate_pairs(values, cosines, sines):
    half_size = values.shape[-1] // 2
    first_half = values[..., :half_size]
    second_half = values[..., half_size:]
    cos_part = cosines[:, None, :]
    sin_part = sines[:, None, :]
    return jnp.concatenate(
        [
            first_half * cos_part - second_half * sin_part,
            second_half * cos_part + first_half * sin_part,
        ],
        axis=-1,
    )


def rotate_back(values, cosines, sines):
    half_size = values.shape[-1] // 2
    first_half = values[..., :half_size]
    second_half = values[..., half_size:]
    cos_part = cosines[:, None, :]
    sin_part = sines[:, None, :]
    return jnp.concatenate(
        [
            first_half * cos_part + second_half * sin_part,
            second_half * cos_part - first_half * sin_part,
        ],
        axis=-1,
    )


def rope_round(values, positions):
    cosines, sines = rotary_tables(positions, HD)
    row_total = values.shape[0]
    return (
        rotate_pairs(values.reshape(row_total, -1, HD), cosines, sines)
        .reshape(row_total, -1)
        .astype(jnp.bfloat16)
    )


def to_blocks(values, n_row, n_seq):
    length, width = values.shape
    return values.reshape(n_row, length // n_row, n_seq, width // n_seq).transpose(0, 2, 1, 3)


def from_blocks(blocks):
    n_row, n_seq, rows, w = blocks.shape
    return blocks.transpose(0, 2, 1, 3).reshape(n_row * rows, n_seq * w)


def project_kernel(lhs_ref, wq_ref, wkv_ref, wo_ref, out_ref):
    feat = wq_ref.shape[0]
    qw = wq_ref.shape[1]
    kw = wkv_ref.shape[1]
    ow = wo_ref.shape[0]
    emb = lhs_ref[:, :feat]
    og = lhs_ref[:, feat:]
    out_ref[:, :qw] = jnp.dot(emb, wq_ref[...], preferred_element_type=jnp.float32)
    out_ref[:, qw : qw + kw] = jnp.dot(emb, wkv_ref[...], preferred_element_type=jnp.float32)
    out_ref[:, qw + kw :] = lax.dot_general(
        og, wo_ref[...], (((1,), (1,)), ((), ())), preferred_element_type=jnp.float32
    )


def project_blocks(lhs, wq, wkv, wo, n_row, n_seq, out_w):
    length, lw = lhs.shape
    feat = wq.shape[0]
    qw = wq.shape[1] // n_seq
    kw = HD
    ow = wo.shape[0] // n_seq
    rows = length // n_row
    flops = 2 * length * feat * (n_seq * (qw + kw + ow))
    return pl.pallas_call(
        project_kernel,
        grid=(n_row, n_seq),
        in_specs=[
            pl.BlockSpec((rows, lw), lambda r, s: (r, 0)),
            pl.BlockSpec((feat, qw), lambda r, s: (0, s)),
            pl.BlockSpec((feat, kw), lambda r, s: (0, s % 2)),
            pl.BlockSpec((ow, feat), lambda r, s: (s, 0)),
        ],
        out_specs=pl.BlockSpec((rows, out_w), lambda r, s: (r * n_seq + s, 0)),
        out_shape=jax.ShapeDtypeStruct((n_row * n_seq * rows, out_w), jnp.float32),
        cost_estimate=pl.CostEstimate(
            flops=flops,
            transcendentals=0,
            bytes_accessed=lhs.size * 2 + (wq.size + wkv.size + wo.size) * 2
            + n_row * n_seq * rows * out_w * 4,
        ),
    )(lhs, wq, wkv, wo)


def attention_kernel(
    q_ref, do_ref, k_ref, v_ref, qpos_ref, qseg_ref, kpos_ref, kseg_ref,
    out_ref, gq_ref, gk_ref, gv_ref,
):
    head = pl.program_id(0)
    score_scale = HD ** (-0.5)
    query = q_ref[0]
    dout = do_ref[0]
    key = k_ref[...]
    value = v_ref[...]
    allowed = (kpos_ref[...] <= qpos_ref[...]) & (kseg_ref[...] == qseg_ref[...])
    nt = (((1,), (1,)), ((), ()))
    tn = (((0,), (0,)), ((), ()))
    raw_scores = (
        lax.dot_general(query, key, nt, preferred_element_type=jnp.float32) * score_scale
    )
    capped = softcap * jnp.tanh(raw_scores / softcap)
    weights = jnp.where(allowed, jnp.exp(capped), 0.0)
    totals = jnp.sum(weights, axis=1, keepdims=True)
    attended = jnp.dot(
        weights.astype(jnp.bfloat16), value, preferred_element_type=jnp.float32
    )
    out_ref[0] = (attended / totals).astype(out_ref.dtype)
    probs = weights / totals
    prob_grads = lax.dot_general(dout, value, nt, preferred_element_type=jnp.float32)
    row_dots = jnp.sum(probs * prob_grads, axis=1, keepdims=True)
    grad_scores = (
        probs * (prob_grads - row_dots) * (1.0 - (capped / softcap) ** 2) * score_scale
    ).astype(jnp.bfloat16)
    gq_ref[0] = jnp.dot(grad_scores, key, preferred_element_type=jnp.float32)
    gk_term = lax.dot_general(grad_scores, query, tn, preferred_element_type=jnp.float32)
    gv_term = lax.dot_general(
        probs.astype(jnp.bfloat16), dout, tn, preferred_element_type=jnp.float32
    )

    @pl.when(head == 0)
    def _():
        gk_ref[...] = gk_term
        gv_ref[...] = gv_term

    @pl.when(head != 0)
    def _():
        gk_ref[...] += gk_term
        gv_ref[...] += gv_term


def attention_block(q, dout, key, value, qpos, qseg, kpos, kseg):
    heads, rows, hd = q.shape
    win = key.shape[0]
    full = lambda h: (0, 0)
    per_head = lambda h: (h, 0, 0)
    return pl.pallas_call(
        attention_kernel,
        grid=(heads,),
        in_specs=[
            pl.BlockSpec((1, rows, hd), per_head),
            pl.BlockSpec((1, rows, hd), per_head),
            pl.BlockSpec((win, hd), full),
            pl.BlockSpec((win, hd), full),
            pl.BlockSpec((rows, 1), full),
            pl.BlockSpec((rows, 1), full),
            pl.BlockSpec((1, win), full),
            pl.BlockSpec((1, win), full),
        ],
        out_specs=[
            pl.BlockSpec((1, rows, hd), per_head),
            pl.BlockSpec((1, rows, hd), per_head),
            pl.BlockSpec((win, hd), full),
            pl.BlockSpec((win, hd), full),
        ],
        out_shape=[
            jax.ShapeDtypeStruct((heads, rows, hd), jnp.bfloat16),
            jax.ShapeDtypeStruct((heads, rows, hd), jnp.float32),
            jax.ShapeDtypeStruct((win, hd), jnp.float32),
            jax.ShapeDtypeStruct((win, hd), jnp.float32),
        ],
        compiler_params=pltpu.CompilerParams(
            dimension_semantics=("arbitrary",), vmem_limit_bytes=48 * 1024 * 1024
        ),
        cost_estimate=pl.CostEstimate(
            flops=12 * heads * rows * win * hd,
            transcendentals=2 * heads * rows * win,
            bytes_accessed=4 * heads * rows * hd * 2 + 4 * win * hd * 4,
        ),
    )(q, dout, key, value, qpos, qseg, kpos, kseg)


def per_device(
    motion_ids,
    audio_ids,
    segment_ids,
    motion_table,
    audio_table,
    norm_gain,
    w_query,
    w_key,
    w_value,
    w_out,
    out_grad,
):
    seq_len = segment_ids.shape[0]
    n_row = lax.axis_size("row")
    n_seq = lax.axis_size("seq")
    n_col = lax.axis_size("col")
    row_index = lax.axis_index("row")
    seq_index = lax.axis_index("seq")
    col_index = lax.axis_index("col")
    n_rs = n_row * n_seq
    block_len = seq_len // n_rs
    quarter_len = seq_len // n_row
    own_len = seq_len // n_col
    feat = motion_table.shape[1]
    query_width = w_query.shape[1]
    kv_width = w_key.shape[1]
    head_count = query_width // HD // n_seq
    part_w = head_count * HD
    score_scale = HD ** (-0.5)
    assert kv_width == HD and part_w == 2 * HD

    embedded = (
        jnp.take(motion_table, motion_ids, axis=0).astype(jnp.float32)
        + jnp.take(audio_table, audio_ids, axis=0).astype(jnp.float32)
    ).astype(jnp.bfloat16)
    residual = embedded.astype(jnp.float32)

    both_all = lax.all_gather(
        jnp.concatenate([embedded, out_grad], axis=1), "col", axis=0, tiled=True
    )
    emb_all = both_all[:, :feat]
    grad_all = both_all[:, feat:]
    emb_all_f = emb_all.astype(jnp.float32)
    gain_col = norm_gain[:, None]
    wq_gain = (w_query.astype(jnp.float32) * gain_col).astype(jnp.bfloat16)
    wkv_gain = (
        jnp.concatenate([w_key, w_value], axis=1).astype(jnp.float32) * gain_col
    ).astype(jnp.bfloat16)
    out_w = part_w + HD + part_w
    squares = lax.psum(lax.psum(jnp.sum(emb_all_f * emb_all_f, axis=1), "seq"), "row")
    inv_all = lax.rsqrt(squares / D + epsilon)
    blocks = project_blocks(both_all, wq_gain, wkv_gain, w_out, n_row, n_seq, out_w)
    got = lax.psum_scatter(blocks, ("row", "seq"), scatter_dimension=0, tiled=True)

    q_raw = got[:, :part_w]
    kv_raw = got[:, part_w : part_w + HD]
    d_raw = got[:, part_w + HD : 2 * part_w + HD]
    inv_q = lax.dynamic_slice(inv_all, (row_index * quarter_len,), (quarter_len,))

    query_pos = row_index * quarter_len + jnp.arange(quarter_len, dtype=jnp.int32)
    queries = rope_round(q_raw * inv_q[:, None], query_pos)
    kv_scaled = kv_raw * inv_q[:, None]
    kv_piece = jnp.where(
        seq_index % 2 == 0, rope_round(kv_scaled, query_pos), kv_scaled.astype(jnp.bfloat16)
    )
    out_heads = d_raw.astype(jnp.bfloat16).reshape(quarter_len, head_count, HD)

    half_len = quarter_len // 2
    kv_half = lax.dynamic_slice(kv_piece, ((seq_index // 2) * half_len, 0), (half_len, HD))
    kv_gath = lax.all_gather(kv_half, ("row", "seq"), axis=0, tiled=True).reshape(
        n_row, 2, 2, half_len, HD
    )
    key_all = kv_gath[:, :, 0].reshape(seq_len, HD)
    value_all = kv_gath[:, :, 1].reshape(seq_len, HD)

    doc_back = -(-(MAX_DOC - 1) // quarter_len) * quarter_len
    win = min(seq_len, quarter_len + doc_back)
    win_start = jnp.clip(row_index * quarter_len - doc_back, 0, seq_len - win)
    key_pos = win_start + jnp.arange(win, dtype=jnp.int32)
    key_sel = lax.dynamic_slice(key_all, (win_start, 0), (win, HD))
    value_sel = lax.dynamic_slice(value_all, (win_start, 0), (win, HD))
    key_seg = lax.dynamic_slice(segment_ids, (win_start,), (win,))
    query_seg = jnp.take(segment_ids, query_pos)
    attn_heads, grad_query_heads, grad_key_part, grad_value_part = attention_block(
        queries.reshape(quarter_len, head_count, HD).transpose(1, 0, 2),
        out_heads.transpose(1, 0, 2),
        key_sel,
        value_sel,
        query_pos[:, None],
        query_seg[:, None],
        key_pos[None, :],
        key_seg[None, :],
    )
    attn_out = attn_heads.transpose(1, 0, 2).reshape(quarter_len, part_w)
    grad_query = grad_query_heads.transpose(1, 0, 2)
    cos_all, sin_all = rotary_tables(key_pos, HD)
    grad_key_rot = rotate_back(grad_key_part[:, None, :], cos_all, sin_all).reshape(
        win, kv_width
    )
    kv_grad_win = jnp.concatenate([grad_key_rot, grad_value_part], axis=1).astype(jnp.bfloat16)
    cos_query, sin_query = rotary_tables(query_pos, HD)
    grad_query_round = (
        rotate_back(grad_query, cos_query, sin_query)
        .reshape(quarter_len, part_w)
        .astype(jnp.bfloat16)
    )
    back_rows = 2 * quarter_len + win + 8
    back_all = lax.all_gather(
        jnp.concatenate(
            [attn_out, grad_query_round, kv_grad_win, jnp.zeros((8, part_w), jnp.bfloat16)], axis=0
        ),
        ("row", "seq"),
        axis=0,
        tiled=True,
    ).reshape(n_rs, back_rows, part_w)
    out_all = from_blocks(back_all[:, :quarter_len].reshape(n_row, n_seq, quarter_len, part_w))
    grad_query_all = from_blocks(
        back_all[:, quarter_len : 2 * quarter_len].reshape(n_row, n_seq, quarter_len, part_w)
    )
    kv_terms = (
        back_all[:, 2 * quarter_len : 2 * quarter_len + win]
        .astype(jnp.float32)
        .reshape(n_row, n_seq, win, part_w)
        .sum(axis=1)
    )
    kv_grad_f = jnp.zeros((seq_len, part_w), jnp.float32)
    for quarter in range(n_row):
        first = min(max(quarter * quarter_len - doc_back, 0), seq_len - win)
        kv_grad_f = kv_grad_f.at[first : first + win].add(kv_terms[quarter])
    kv_grad_all = kv_grad_f.astype(jnp.bfloat16)

    normed_all = (emb_all_f * inv_all[:, None] * norm_gain[None, :]).astype(jnp.bfloat16)
    grad_wo = jnp.einsum("ln,ld->nd", out_all, grad_all, preferred_element_type=jnp.float32)
    grad_wq = jnp.einsum(
        "ld,ln->dn", normed_all, grad_query_all, preferred_element_type=jnp.float32
    )
    grad_wk = jnp.einsum(
        "ld,ln->dn", normed_all, kv_grad_all[:, :kv_width], preferred_element_type=jnp.float32
    )
    grad_wv = jnp.einsum(
        "ld,ln->dn", normed_all, kv_grad_all[:, kv_width:], preferred_element_type=jnp.float32
    )

    branch_part = jnp.dot(out_all, w_out, preferred_element_type=jnp.float32)
    total_term = jnp.einsum(
        "ln,dn->ld", grad_query_all, w_query, preferred_element_type=jnp.float32
    )
    total_term = total_term + jnp.einsum(
        "ln,dn->ld", kv_grad_all[:, :kv_width], w_key, preferred_element_type=jnp.float32
    )
    total_term = total_term + jnp.einsum(
        "ln,dn->ld", kv_grad_all[:, kv_width:], w_value, preferred_element_type=jnp.float32
    )
    emb_inv_all = emb_all_f * inv_all[:, None]
    gain_terms = jnp.sum(total_term * emb_inv_all, axis=0)
    dot_terms = jnp.sum(total_term * (emb_all_f * norm_gain[None, :]), axis=1)
    col_terms = lax.psum(jnp.concatenate([gain_terms, dot_terms]), "col")
    grad_gain = col_terms[:feat]
    own_dots = lax.dynamic_slice(col_terms[feat:], (col_index * own_len,), (own_len,))
    total_dot = lax.psum(lax.psum(own_dots, "seq"), "row")
    col_sum = lax.psum_scatter(
        jnp.concatenate([branch_part, total_term], axis=1).astype(jnp.bfloat16),
        "col",
        scatter_dimension=0,
        tiled=True,
    ).astype(jnp.float32)
    branch_sum = col_sum[:, :feat]
    grad_normed = col_sum[:, feat:]
    layer_out = (residual + branch_sum).astype(jnp.bfloat16)

    inverse = lax.dynamic_slice(inv_all, (col_index * own_len,), (own_len,))
    scaled_grad = grad_normed * norm_gain[None, :]
    grad_input = (
        out_grad.astype(jnp.float32)
        + inverse[:, None] * scaled_grad
        - residual * (inverse**3 * total_dot / D)[:, None]
    ).astype(jnp.bfloat16)
    return (layer_out, grad_input, grad_gain, grad_wq, grad_wk, grad_wv, grad_wo)


def solution(mesh):
    placed = (
        P("col"),
        P("col"),
        P(),
        P(None, ("row", "seq")),
        P(None, ("row", "seq")),
        P(("row", "seq")),
        P(("row", "seq"), "col"),
        P(("row", "seq"), "col"),
        P(("row", "seq"), "col"),
        P("col", ("row", "seq")),
        P("col", ("row", "seq")),
    )
    return jax.shard_map(
        per_device,
        mesh=mesh,
        in_specs=placed,
        out_specs=(
            P("col", ("row", "seq")),
            P("col", ("row", "seq")),
            P(("row", "seq")),
            P(("row", "seq"), "col"),
            P(("row", "seq"), "col"),
            P(("row", "seq"), "col"),
            P("col", ("row", "seq")),
        ),
        check_vma=False,
    )
```

```python
import jax
import jax.numpy as jnp
from jax import lax
from jax.sharding import PartitionSpec as P
from jax.experimental import pallas as pl
from jax.experimental.pallas import tpu as pltpu

D = 8192
H = 64
KV = 8
HD = 128


epsilon = 1e-05
softcap = 20.0
rope_base = 500000.0
MAX_DOC = 768


def rotary_tables(positions, head_size):
    half_size = head_size // 2
    frequency = rope_base ** (-(jnp.arange(half_size, dtype=jnp.float32) * 2.0) / head_size)
    angles = positions.astype(jnp.float32)[:, None] * frequency[None, :]
    return (jnp.cos(angles), jnp.sin(angles))


def rotate_pairs(values, cosines, sines):
    half_size = values.shape[-1] // 2
    first_half = values[..., :half_size]
    second_half = values[..., half_size:]
    cos_part = cosines[:, None, :]
    sin_part = sines[:, None, :]
    return jnp.concatenate(
        [
            first_half * cos_part - second_half * sin_part,
            second_half * cos_part + first_half * sin_part,
        ],
        axis=-1,
    )


def rotate_back(values, cosines, sines):
    half_size = values.shape[-1] // 2
    first_half = values[..., :half_size]
    second_half = values[..., half_size:]
    cos_part = cosines[:, None, :]
    sin_part = sines[:, None, :]
    return jnp.concatenate(
        [
            first_half * cos_part + second_half * sin_part,
            second_half * cos_part - first_half * sin_part,
        ],
        axis=-1,
    )


def rope_round(values, positions):
    cosines, sines = rotary_tables(positions, HD)
    row_total = values.shape[0]
    return (
        rotate_pairs(values.reshape(row_total, -1, HD), cosines, sines)
        .reshape(row_total, -1)
        .astype(jnp.bfloat16)
    )


def to_blocks(values, n_row, n_seq):
    length, width = values.shape
    return values.reshape(n_row, length // n_row, n_seq, width // n_seq).transpose(0, 2, 1, 3)


def from_blocks(blocks):
    n_row, n_seq, rows, w = blocks.shape
    return blocks.transpose(0, 2, 1, 3).reshape(n_row * rows, n_seq * w)


def project_kernel(lhs_ref, wq_ref, wkv_ref, wo_ref, out_ref):
    feat = wq_ref.shape[0]
    qw = wq_ref.shape[1]
    kw = wkv_ref.shape[1]
    n_row, _, rows, _ = out_ref.shape
    for r in range(n_row):
        emb = lhs_ref[r * rows : (r + 1) * rows, :feat]
        og = lhs_ref[r * rows : (r + 1) * rows, feat:]
        out_ref[r, 0, :, :qw] = jnp.dot(emb, wq_ref[...], preferred_element_type=jnp.float32)
        out_ref[r, 0, :, qw : qw + kw] = jnp.dot(
            emb, wkv_ref[...], preferred_element_type=jnp.float32
        )
        out_ref[r, 0, :, qw + kw :] = lax.dot_general(
            og, wo_ref[...], (((1,), (1,)), ((), ())), preferred_element_type=jnp.float32
        )


def project_blocks(lhs, wq, wkv, wo, n_row, n_seq, out_w):
    length, lw = lhs.shape
    feat = wq.shape[0]
    qw = wq.shape[1] // n_seq
    kw = HD
    ow = wo.shape[0] // n_seq
    rows = length // n_row
    flops = 2 * length * feat * (n_seq * (qw + kw + ow))
    out = pl.pallas_call(
        project_kernel,
        grid=(n_seq,),
        in_specs=[
            pl.BlockSpec((length, lw), lambda s: (0, 0)),
            pl.BlockSpec((feat, qw), lambda s: (0, s)),
            pl.BlockSpec((feat, kw), lambda s: (0, s % 2)),
            pl.BlockSpec((ow, feat), lambda s: (s, 0)),
        ],
        out_specs=pl.BlockSpec((n_row, 1, rows, out_w), lambda s: (0, s, 0, 0)),
        out_shape=jax.ShapeDtypeStruct((n_row, n_seq, rows, out_w), jnp.float32),
        compiler_params=pltpu.CompilerParams(vmem_limit_bytes=48 * 1024 * 1024),
        cost_estimate=pl.CostEstimate(
            flops=flops,
            transcendentals=0,
            bytes_accessed=lhs.size * 2 + (wq.size + wkv.size + wo.size) * 2
            + n_row * n_seq * rows * out_w * 4,
        ),
    )(lhs, wq, wkv, wo)
    return out.reshape(n_row * n_seq * rows, out_w)


def attention_kernel(
    q_ref, do_ref, k_ref, v_ref, qpos_ref, qseg_ref, kpos_ref, kseg_ref,
    out_ref, gq_ref, gk_ref, gv_ref,
):
    head = pl.program_id(0)
    score_scale = HD ** (-0.5)
    query = q_ref[0]
    dout = do_ref[0]
    key = k_ref[...]
    value = v_ref[...]
    allowed = (kpos_ref[...] <= qpos_ref[...]) & (kseg_ref[...] == qseg_ref[...])
    nt = (((1,), (1,)), ((), ()))
    tn = (((0,), (0,)), ((), ()))
    raw_scores = (
        lax.dot_general(query, key, nt, preferred_element_type=jnp.float32) * score_scale
    )
    capped = softcap * jnp.tanh(raw_scores / softcap)
    weights = jnp.where(allowed, jnp.exp(capped), 0.0)
    totals = jnp.sum(weights, axis=1, keepdims=True)
    attended = jnp.dot(
        weights.astype(jnp.bfloat16), value, preferred_element_type=jnp.float32
    )
    out_ref[0] = (attended / totals).astype(out_ref.dtype)
    probs = weights / totals
    prob_grads = lax.dot_general(dout, value, nt, preferred_element_type=jnp.float32)
    row_dots = jnp.sum(probs * prob_grads, axis=1, keepdims=True)
    grad_scores = (
        probs * (prob_grads - row_dots) * (1.0 - (capped / softcap) ** 2) * score_scale
    ).astype(jnp.bfloat16)
    gq_ref[0] = jnp.dot(grad_scores, key, preferred_element_type=jnp.float32)
    gk_term = lax.dot_general(grad_scores, query, tn, preferred_element_type=jnp.float32)
    gv_term = lax.dot_general(
        probs.astype(jnp.bfloat16), dout, tn, preferred_element_type=jnp.float32
    )

    @pl.when(head == 0)
    def _():
        gk_ref[...] = gk_term
        gv_ref[...] = gv_term

    @pl.when(head != 0)
    def _():
        gk_ref[...] += gk_term
        gv_ref[...] += gv_term


def attention_block(q, dout, key, value, qpos, qseg, kpos, kseg):
    heads, rows, hd = q.shape
    win = key.shape[0]
    full = lambda h: (0, 0)
    per_head = lambda h: (h, 0, 0)
    return pl.pallas_call(
        attention_kernel,
        grid=(heads,),
        in_specs=[
            pl.BlockSpec((1, rows, hd), per_head),
            pl.BlockSpec((1, rows, hd), per_head),
            pl.BlockSpec((win, hd), full),
            pl.BlockSpec((win, hd), full),
            pl.BlockSpec((rows, 1), full),
            pl.BlockSpec((rows, 1), full),
            pl.BlockSpec((1, win), full),
            pl.BlockSpec((1, win), full),
        ],
        out_specs=[
            pl.BlockSpec((1, rows, hd), per_head),
            pl.BlockSpec((1, rows, hd), per_head),
            pl.BlockSpec((win, hd), full),
            pl.BlockSpec((win, hd), full),
        ],
        out_shape=[
            jax.ShapeDtypeStruct((heads, rows, hd), jnp.bfloat16),
            jax.ShapeDtypeStruct((heads, rows, hd), jnp.float32),
            jax.ShapeDtypeStruct((win, hd), jnp.float32),
            jax.ShapeDtypeStruct((win, hd), jnp.float32),
        ],
        compiler_params=pltpu.CompilerParams(
            dimension_semantics=("arbitrary",), vmem_limit_bytes=48 * 1024 * 1024
        ),
        cost_estimate=pl.CostEstimate(
            flops=12 * heads * rows * win * hd,
            transcendentals=2 * heads * rows * win,
            bytes_accessed=4 * heads * rows * hd * 2 + 4 * win * hd * 4,
        ),
    )(q, dout, key, value, qpos, qseg, kpos, kseg)


def per_device(
    motion_ids,
    audio_ids,
    segment_ids,
    motion_table,
    audio_table,
    norm_gain,
    w_query,
    w_key,
    w_value,
    w_out,
    out_grad,
):
    seq_len = segment_ids.shape[0]
    n_row = lax.axis_size("row")
    n_seq = lax.axis_size("seq")
    n_col = lax.axis_size("col")
    row_index = lax.axis_index("row")
    seq_index = lax.axis_index("seq")
    col_index = lax.axis_index("col")
    n_rs = n_row * n_seq
    block_len = seq_len // n_rs
    quarter_len = seq_len // n_row
    own_len = seq_len // n_col
    feat = motion_table.shape[1]
    query_width = w_query.shape[1]
    kv_width = w_key.shape[1]
    head_count = query_width // HD // n_seq
    part_w = head_count * HD
    score_scale = HD ** (-0.5)
    assert kv_width == HD and part_w == 2 * HD

    embedded = (
        jnp.take(motion_table, motion_ids, axis=0).astype(jnp.float32)
        + jnp.take(audio_table, audio_ids, axis=0).astype(jnp.float32)
    ).astype(jnp.bfloat16)
    residual = embedded.astype(jnp.float32)

    both_all = lax.all_gather(
        jnp.concatenate([embedded, out_grad], axis=1), "col", axis=0, tiled=True
    )
    emb_all = both_all[:, :feat]
    grad_all = both_all[:, feat:]
    emb_all_f = emb_all.astype(jnp.float32)
    gain_col = norm_gain[:, None]
    wq_gain = (w_query.astype(jnp.float32) * gain_col).astype(jnp.bfloat16)
    wkv_gain = (
        jnp.concatenate([w_key, w_value], axis=1).astype(jnp.float32) * gain_col
    ).astype(jnp.bfloat16)
    out_w = part_w + HD + part_w
    squares = lax.psum(lax.psum(jnp.sum(emb_all_f * emb_all_f, axis=1), "seq"), "row")
    inv_all = lax.rsqrt(squares / D + epsilon)
    blocks = project_blocks(both_all, wq_gain, wkv_gain, w_out, n_row, n_seq, out_w)
    got = lax.psum_scatter(blocks, ("row", "seq"), scatter_dimension=0, tiled=True)

    q_raw = got[:, :part_w]
    kv_raw = got[:, part_w : part_w + HD]
    d_raw = got[:, part_w + HD : 2 * part_w + HD]
    inv_q = lax.dynamic_slice(inv_all, (row_index * quarter_len,), (quarter_len,))

    query_pos = row_index * quarter_len + jnp.arange(quarter_len, dtype=jnp.int32)
    queries = rope_round(q_raw * inv_q[:, None], query_pos)
    kv_scaled = kv_raw * inv_q[:, None]
    kv_piece = jnp.where(
        seq_index % 2 == 0, rope_round(kv_scaled, query_pos), kv_scaled.astype(jnp.bfloat16)
    )
    out_heads = d_raw.astype(jnp.bfloat16).reshape(quarter_len, head_count, HD)

    half_len = quarter_len // 2
    kv_half = lax.dynamic_slice(kv_piece, ((seq_index // 2) * half_len, 0), (half_len, HD))
    kv_gath = lax.all_gather(kv_half, ("row", "seq"), axis=0, tiled=True).reshape(
        n_row, 2, 2, half_len, HD
    )
    key_all = kv_gath[:, :, 0].reshape(seq_len, HD)
    value_all = kv_gath[:, :, 1].reshape(seq_len, HD)

    doc_back = -(-(MAX_DOC - 1) // quarter_len) * quarter_len
    win = min(seq_len, quarter_len + doc_back)
    win_start = jnp.clip(row_index * quarter_len - doc_back, 0, seq_len - win)
    key_pos = win_start + jnp.arange(win, dtype=jnp.int32)
    key_sel = lax.dynamic_slice(key_all, (win_start, 0), (win, HD))
    value_sel = lax.dynamic_slice(value_all, (win_start, 0), (win, HD))
    key_seg = lax.dynamic_slice(segment_ids, (win_start,), (win,))
    query_seg = jnp.take(segment_ids, query_pos)
    attn_heads, grad_query_heads, grad_key_part, grad_value_part = attention_block(
        queries.reshape(quarter_len, head_count, HD).transpose(1, 0, 2),
        out_heads.transpose(1, 0, 2),
        key_sel,
        value_sel,
        query_pos[:, None],
        query_seg[:, None],
        key_pos[None, :],
        key_seg[None, :],
    )
    attn_out = attn_heads.transpose(1, 0, 2).reshape(quarter_len, part_w)
    grad_query = grad_query_heads.transpose(1, 0, 2)
    cos_all, sin_all = rotary_tables(key_pos, HD)
    grad_key_rot = rotate_back(grad_key_part[:, None, :], cos_all, sin_all).reshape(
        win, kv_width
    )
    kv_grad_win = jnp.concatenate([grad_key_rot, grad_value_part], axis=1).astype(jnp.bfloat16)
    cos_query, sin_query = rotary_tables(query_pos, HD)
    grad_query_round = (
        rotate_back(grad_query, cos_query, sin_query)
        .reshape(quarter_len, part_w)
        .astype(jnp.bfloat16)
    )
    back_rows = 2 * quarter_len + win + 8
    back_all = lax.all_gather(
        jnp.concatenate(
            [attn_out, grad_query_round, kv_grad_win, jnp.zeros((8, part_w), jnp.bfloat16)], axis=0
        ),
        ("row", "seq"),
        axis=0,
        tiled=True,
    ).reshape(n_rs, back_rows, part_w)
    out_all = from_blocks(back_all[:, :quarter_len].reshape(n_row, n_seq, quarter_len, part_w))
    grad_query_all = from_blocks(
        back_all[:, quarter_len : 2 * quarter_len].reshape(n_row, n_seq, quarter_len, part_w)
    )
    kv_terms = (
        back_all[:, 2 * quarter_len : 2 * quarter_len + win]
        .astype(jnp.float32)
        .reshape(n_row, n_seq, win, part_w)
        .sum(axis=1)
    )
    kv_grad_f = jnp.zeros((seq_len, part_w), jnp.float32)
    for quarter in range(n_row):
        first = min(max(quarter * quarter_len - doc_back, 0), seq_len - win)
        kv_grad_f = kv_grad_f.at[first : first + win].add(kv_terms[quarter])
    kv_grad_all = kv_grad_f.astype(jnp.bfloat16)

    normed_all = (emb_all_f * inv_all[:, None] * norm_gain[None, :]).astype(jnp.bfloat16)
    grad_wo = jnp.einsum("ln,ld->nd", out_all, grad_all, preferred_element_type=jnp.float32)
    grad_wq = jnp.einsum(
        "ld,ln->dn", normed_all, grad_query_all, preferred_element_type=jnp.float32
    )
    grad_wk = jnp.einsum(
        "ld,ln->dn", normed_all, kv_grad_all[:, :kv_width], preferred_element_type=jnp.float32
    )
    grad_wv = jnp.einsum(
        "ld,ln->dn", normed_all, kv_grad_all[:, kv_width:], preferred_element_type=jnp.float32
    )

    branch_part = jnp.dot(out_all, w_out, preferred_element_type=jnp.float32)
    total_term = jnp.einsum(
        "ln,dn->ld", grad_query_all, w_query, preferred_element_type=jnp.float32
    )
    total_term = total_term + jnp.einsum(
        "ln,dn->ld", kv_grad_all[:, :kv_width], w_key, preferred_element_type=jnp.float32
    )
    total_term = total_term + jnp.einsum(
        "ln,dn->ld", kv_grad_all[:, kv_width:], w_value, preferred_element_type=jnp.float32
    )
    emb_inv_all = emb_all_f * inv_all[:, None]
    gain_terms = jnp.sum(total_term * emb_inv_all, axis=0)
    dot_terms = jnp.sum(total_term * (emb_all_f * norm_gain[None, :]), axis=1)
    col_terms = lax.psum(jnp.concatenate([gain_terms, dot_terms]), "col")
    grad_gain = col_terms[:feat]
    own_dots = lax.dynamic_slice(col_terms[feat:], (col_index * own_len,), (own_len,))
    total_dot = lax.psum(lax.psum(own_dots, "seq"), "row")
    col_sum = lax.psum_scatter(
        jnp.concatenate([branch_part, total_term], axis=1).astype(jnp.bfloat16),
        "col",
        scatter_dimension=0,
        tiled=True,
    ).astype(jnp.float32)
    branch_sum = col_sum[:, :feat]
    grad_normed = col_sum[:, feat:]
    layer_out = (residual + branch_sum).astype(jnp.bfloat16)

    inverse = lax.dynamic_slice(inv_all, (col_index * own_len,), (own_len,))
    scaled_grad = grad_normed * norm_gain[None, :]
    grad_input = (
        out_grad.astype(jnp.float32)
        + inverse[:, None] * scaled_grad
        - residual * (inverse**3 * total_dot / D)[:, None]
    ).astype(jnp.bfloat16)
    return (layer_out, grad_input, grad_gain, grad_wq, grad_wk, grad_wv, grad_wo)


def solution(mesh):
    placed = (
        P("col"),
        P("col"),
        P(),
        P(None, ("row", "seq")),
        P(None, ("row", "seq")),
        P(("row", "seq")),
        P(("row", "seq"), "col"),
        P(("row", "seq"), "col"),
        P(("row", "seq"), "col"),
        P("col", ("row", "seq")),
        P("col", ("row", "seq")),
    )
    return jax.shard_map(
        per_device,
        mesh=mesh,
        in_specs=placed,
        out_specs=(
            P("col", ("row", "seq")),
            P("col", ("row", "seq")),
            P(("row", "seq")),
            P(("row", "seq"), "col"),
            P(("row", "seq"), "col"),
            P(("row", "seq"), "col"),
            P("col", ("row", "seq")),
        ),
        check_vma=False,
    )
```

```python
import jax
import jax.numpy as jnp
from jax import lax
from jax.sharding import PartitionSpec as P
from jax.experimental import pallas as pl
from jax.experimental.pallas import tpu as pltpu

D = 8192
H = 64
KV = 8
HD = 128


epsilon = 1e-05
softcap = 20.0
rope_base = 500000.0
MAX_DOC = 768


def rotary_tables(positions, head_size):
    half_size = head_size // 2
    frequency = rope_base ** (-(jnp.arange(half_size, dtype=jnp.float32) * 2.0) / head_size)
    angles = positions.astype(jnp.float32)[:, None] * frequency[None, :]
    return (jnp.cos(angles), jnp.sin(angles))


def rotate_pairs(values, cosines, sines):
    half_size = values.shape[-1] // 2
    first_half = values[..., :half_size]
    second_half = values[..., half_size:]
    cos_part = cosines[:, None, :]
    sin_part = sines[:, None, :]
    return jnp.concatenate(
        [
            first_half * cos_part - second_half * sin_part,
            second_half * cos_part + first_half * sin_part,
        ],
        axis=-1,
    )


def rotate_back(values, cosines, sines):
    half_size = values.shape[-1] // 2
    first_half = values[..., :half_size]
    second_half = values[..., half_size:]
    cos_part = cosines[:, None, :]
    sin_part = sines[:, None, :]
    return jnp.concatenate(
        [
            first_half * cos_part + second_half * sin_part,
            second_half * cos_part - first_half * sin_part,
        ],
        axis=-1,
    )


def rope_round(values, positions):
    cosines, sines = rotary_tables(positions, HD)
    row_total = values.shape[0]
    return (
        rotate_pairs(values.reshape(row_total, -1, HD), cosines, sines)
        .reshape(row_total, -1)
        .astype(jnp.bfloat16)
    )


def to_blocks(values, n_row, n_seq):
    length, width = values.shape
    return values.reshape(n_row, length // n_row, n_seq, width // n_seq).transpose(0, 2, 1, 3)


def from_blocks(blocks):
    n_row, n_seq, rows, w = blocks.shape
    return blocks.transpose(0, 2, 1, 3).reshape(n_row * rows, n_seq * w)


def project_kernel(lhs_ref, wq_ref, wkv_ref, wo_ref, out_hbm, buf, sems):
    part = pl.program_id(0)
    n_part = pl.num_programs(0)
    feat = wq_ref.shape[0]
    qw = wq_ref.shape[1]
    kw = wkv_ref.shape[1]
    n_row, rows, _ = buf.shape
    copies = []
    for r in range(n_row):
        emb = lhs_ref[r * rows : (r + 1) * rows, :feat]
        og = lhs_ref[r * rows : (r + 1) * rows, feat:]
        buf[r, :, :qw] = jnp.dot(emb, wq_ref[...], preferred_element_type=jnp.float32)
        buf[r, :, qw : qw + kw] = jnp.dot(emb, wkv_ref[...], preferred_element_type=jnp.float32)
        buf[r, :, qw + kw :] = lax.dot_general(
            og, wo_ref[...], (((1,), (1,)), ((), ())), preferred_element_type=jnp.float32
        )
        copy = pltpu.make_async_copy(
            buf.at[r], out_hbm.at[pl.ds((r * n_part + part) * rows, rows)], sems.at[r]
        )
        copy.start()
        copies.append(copy)
    for copy in copies:
        copy.wait()


def project_blocks(lhs, wq, wkv, wo, n_row, n_seq, out_w):
    length, lw = lhs.shape
    feat = wq.shape[0]
    qw = wq.shape[1] // n_seq
    kw = HD
    ow = wo.shape[0] // n_seq
    rows = length // n_row
    flops = 2 * length * feat * (n_seq * (qw + kw + ow))
    return pl.pallas_call(
        project_kernel,
        grid=(n_seq,),
        in_specs=[
            pl.BlockSpec((length, lw), lambda s: (0, 0)),
            pl.BlockSpec((feat, qw), lambda s: (0, s)),
            pl.BlockSpec((feat, kw), lambda s: (0, s % 2)),
            pl.BlockSpec((ow, feat), lambda s: (s, 0)),
        ],
        out_specs=pl.BlockSpec(memory_space=pl.ANY),
        out_shape=jax.ShapeDtypeStruct((n_row * n_seq * rows, out_w), jnp.float32),
        scratch_shapes=[
            pltpu.VMEM((n_row, rows, out_w), jnp.float32),
            pltpu.SemaphoreType.DMA((n_row,)),
        ],
        compiler_params=pltpu.CompilerParams(vmem_limit_bytes=48 * 1024 * 1024),
        cost_estimate=pl.CostEstimate(
            flops=flops,
            transcendentals=0,
            bytes_accessed=lhs.size * 2 + (wq.size + wkv.size + wo.size) * 2
            + n_row * n_seq * rows * out_w * 4,
        ),
    )(lhs, wq, wkv, wo)


def attention_kernel(
    q_ref, do_ref, k_ref, v_ref, qpos_ref, qseg_ref, kpos_ref, kseg_ref,
    out_ref, gq_ref, gk_ref, gv_ref,
):
    head = pl.program_id(0)
    score_scale = HD ** (-0.5)
    query = q_ref[0]
    dout = do_ref[0]
    key = k_ref[...]
    value = v_ref[...]
    allowed = (kpos_ref[...] <= qpos_ref[...]) & (kseg_ref[...] == qseg_ref[...])
    nt = (((1,), (1,)), ((), ()))
    tn = (((0,), (0,)), ((), ()))
    raw_scores = (
        lax.dot_general(query, key, nt, preferred_element_type=jnp.float32) * score_scale
    )
    capped = softcap * jnp.tanh(raw_scores / softcap)
    weights = jnp.where(allowed, jnp.exp(capped), 0.0)
    totals = jnp.sum(weights, axis=1, keepdims=True)
    attended = jnp.dot(
        weights.astype(jnp.bfloat16), value, preferred_element_type=jnp.float32
    )
    out_ref[0] = (attended / totals).astype(out_ref.dtype)
    probs = weights / totals
    prob_grads = lax.dot_general(dout, value, nt, preferred_element_type=jnp.float32)
    row_dots = jnp.sum(probs * prob_grads, axis=1, keepdims=True)
    grad_scores = (
        probs * (prob_grads - row_dots) * (1.0 - (capped / softcap) ** 2) * score_scale
    ).astype(jnp.bfloat16)
    gq_ref[0] = jnp.dot(grad_scores, key, preferred_element_type=jnp.float32)
    gk_term = lax.dot_general(grad_scores, query, tn, preferred_element_type=jnp.float32)
    gv_term = lax.dot_general(
        probs.astype(jnp.bfloat16), dout, tn, preferred_element_type=jnp.float32
    )

    @pl.when(head == 0)
    def _():
        gk_ref[...] = gk_term
        gv_ref[...] = gv_term

    @pl.when(head != 0)
    def _():
        gk_ref[...] += gk_term
        gv_ref[...] += gv_term


def attention_block(q, dout, key, value, qpos, qseg, kpos, kseg):
    heads, rows, hd = q.shape
    win = key.shape[0]
    full = lambda h: (0, 0)
    per_head = lambda h: (h, 0, 0)
    return pl.pallas_call(
        attention_kernel,
        grid=(heads,),
        in_specs=[
            pl.BlockSpec((1, rows, hd), per_head),
            pl.BlockSpec((1, rows, hd), per_head),
            pl.BlockSpec((win, hd), full),
            pl.BlockSpec((win, hd), full),
            pl.BlockSpec((rows, 1), full),
            pl.BlockSpec((rows, 1), full),
            pl.BlockSpec((1, win), full),
            pl.BlockSpec((1, win), full),
        ],
        out_specs=[
            pl.BlockSpec((1, rows, hd), per_head),
            pl.BlockSpec((1, rows, hd), per_head),
            pl.BlockSpec((win, hd), full),
            pl.BlockSpec((win, hd), full),
        ],
        out_shape=[
            jax.ShapeDtypeStruct((heads, rows, hd), jnp.bfloat16),
            jax.ShapeDtypeStruct((heads, rows, hd), jnp.float32),
            jax.ShapeDtypeStruct((win, hd), jnp.float32),
            jax.ShapeDtypeStruct((win, hd), jnp.float32),
        ],
        compiler_params=pltpu.CompilerParams(
            dimension_semantics=("arbitrary",), vmem_limit_bytes=48 * 1024 * 1024
        ),
        cost_estimate=pl.CostEstimate(
            flops=12 * heads * rows * win * hd,
            transcendentals=2 * heads * rows * win,
            bytes_accessed=4 * heads * rows * hd * 2 + 4 * win * hd * 4,
        ),
    )(q, dout, key, value, qpos, qseg, kpos, kseg)


def per_device(
    motion_ids,
    audio_ids,
    segment_ids,
    motion_table,
    audio_table,
    norm_gain,
    w_query,
    w_key,
    w_value,
    w_out,
    out_grad,
):
    seq_len = segment_ids.shape[0]
    n_row = lax.axis_size("row")
    n_seq = lax.axis_size("seq")
    n_col = lax.axis_size("col")
    row_index = lax.axis_index("row")
    seq_index = lax.axis_index("seq")
    col_index = lax.axis_index("col")
    n_rs = n_row * n_seq
    block_len = seq_len // n_rs
    quarter_len = seq_len // n_row
    own_len = seq_len // n_col
    feat = motion_table.shape[1]
    query_width = w_query.shape[1]
    kv_width = w_key.shape[1]
    head_count = query_width // HD // n_seq
    part_w = head_count * HD
    score_scale = HD ** (-0.5)
    assert kv_width == HD and part_w == 2 * HD

    embedded = (
        jnp.take(motion_table, motion_ids, axis=0).astype(jnp.float32)
        + jnp.take(audio_table, audio_ids, axis=0).astype(jnp.float32)
    ).astype(jnp.bfloat16)
    residual = embedded.astype(jnp.float32)

    both_all = lax.all_gather(
        jnp.concatenate([embedded, out_grad], axis=1), "col", axis=0, tiled=True
    )
    emb_all = both_all[:, :feat]
    grad_all = both_all[:, feat:]
    emb_all_f = emb_all.astype(jnp.float32)
    gain_col = norm_gain[:, None]
    wq_gain = (w_query.astype(jnp.float32) * gain_col).astype(jnp.bfloat16)
    wkv_gain = (
        jnp.concatenate([w_key, w_value], axis=1).astype(jnp.float32) * gain_col
    ).astype(jnp.bfloat16)
    out_w = part_w + HD + part_w
    squares = lax.psum(lax.psum(jnp.sum(emb_all_f * emb_all_f, axis=1), "seq"), "row")
    inv_all = lax.rsqrt(squares / D + epsilon)
    blocks = project_blocks(both_all, wq_gain, wkv_gain, w_out, n_row, n_seq, out_w)
    got = lax.psum_scatter(blocks, ("row", "seq"), scatter_dimension=0, tiled=True)

    q_raw = got[:, :part_w]
    kv_raw = got[:, part_w : part_w + HD]
    d_raw = got[:, part_w + HD : 2 * part_w + HD]
    inv_q = lax.dynamic_slice(inv_all, (row_index * quarter_len,), (quarter_len,))

    query_pos = row_index * quarter_len + jnp.arange(quarter_len, dtype=jnp.int32)
    queries = rope_round(q_raw * inv_q[:, None], query_pos)
    kv_scaled = kv_raw * inv_q[:, None]
    kv_piece = jnp.where(
        seq_index % 2 == 0, rope_round(kv_scaled, query_pos), kv_scaled.astype(jnp.bfloat16)
    )
    out_heads = d_raw.astype(jnp.bfloat16).reshape(quarter_len, head_count, HD)

    half_len = quarter_len // 2
    kv_half = lax.dynamic_slice(kv_piece, ((seq_index // 2) * half_len, 0), (half_len, HD))
    kv_gath = lax.all_gather(kv_half, ("row", "seq"), axis=0, tiled=True).reshape(
        n_row, 2, 2, half_len, HD
    )
    key_all = kv_gath[:, :, 0].reshape(seq_len, HD)
    value_all = kv_gath[:, :, 1].reshape(seq_len, HD)

    doc_back = -(-(MAX_DOC - 1) // quarter_len) * quarter_len
    win = min(seq_len, quarter_len + doc_back)
    win_start = jnp.clip(row_index * quarter_len - doc_back, 0, seq_len - win)
    key_pos = win_start + jnp.arange(win, dtype=jnp.int32)
    key_sel = lax.dynamic_slice(key_all, (win_start, 0), (win, HD))
    value_sel = lax.dynamic_slice(value_all, (win_start, 0), (win, HD))
    key_seg = lax.dynamic_slice(segment_ids, (win_start,), (win,))
    query_seg = jnp.take(segment_ids, query_pos)
    attn_heads, grad_query_heads, grad_key_part, grad_value_part = attention_block(
        queries.reshape(quarter_len, head_count, HD).transpose(1, 0, 2),
        out_heads.transpose(1, 0, 2),
        key_sel,
        value_sel,
        query_pos[:, None],
        query_seg[:, None],
        key_pos[None, :],
        key_seg[None, :],
    )
    attn_out = attn_heads.transpose(1, 0, 2).reshape(quarter_len, part_w)
    grad_query = grad_query_heads.transpose(1, 0, 2)
    cos_all, sin_all = rotary_tables(key_pos, HD)
    grad_key_rot = rotate_back(grad_key_part[:, None, :], cos_all, sin_all).reshape(
        win, kv_width
    )
    kv_grad_win = jnp.concatenate([grad_key_rot, grad_value_part], axis=1).astype(jnp.bfloat16)
    cos_query, sin_query = rotary_tables(query_pos, HD)
    grad_query_round = (
        rotate_back(grad_query, cos_query, sin_query)
        .reshape(quarter_len, part_w)
        .astype(jnp.bfloat16)
    )
    back_rows = 2 * quarter_len + win + 8
    back_all = lax.all_gather(
        jnp.concatenate(
            [attn_out, grad_query_round, kv_grad_win, jnp.zeros((8, part_w), jnp.bfloat16)], axis=0
        ),
        ("row", "seq"),
        axis=0,
        tiled=True,
    ).reshape(n_rs, back_rows, part_w)
    out_all = from_blocks(back_all[:, :quarter_len].reshape(n_row, n_seq, quarter_len, part_w))
    grad_query_all = from_blocks(
        back_all[:, quarter_len : 2 * quarter_len].reshape(n_row, n_seq, quarter_len, part_w)
    )
    kv_terms = (
        back_all[:, 2 * quarter_len : 2 * quarter_len + win]
        .astype(jnp.float32)
        .reshape(n_row, n_seq, win, part_w)
        .sum(axis=1)
    )
    kv_grad_f = jnp.zeros((seq_len, part_w), jnp.float32)
    for quarter in range(n_row):
        first = min(max(quarter * quarter_len - doc_back, 0), seq_len - win)
        kv_grad_f = kv_grad_f.at[first : first + win].add(kv_terms[quarter])
    kv_grad_all = kv_grad_f.astype(jnp.bfloat16)

    normed_all = (emb_all_f * inv_all[:, None] * norm_gain[None, :]).astype(jnp.bfloat16)
    grad_wo = jnp.einsum("ln,ld->nd", out_all, grad_all, preferred_element_type=jnp.float32)
    grad_wq = jnp.einsum(
        "ld,ln->dn", normed_all, grad_query_all, preferred_element_type=jnp.float32
    )
    grad_wk = jnp.einsum(
        "ld,ln->dn", normed_all, kv_grad_all[:, :kv_width], preferred_element_type=jnp.float32
    )
    grad_wv = jnp.einsum(
        "ld,ln->dn", normed_all, kv_grad_all[:, kv_width:], preferred_element_type=jnp.float32
    )

    branch_part = jnp.dot(out_all, w_out, preferred_element_type=jnp.float32)
    total_term = jnp.einsum(
        "ln,dn->ld", grad_query_all, w_query, preferred_element_type=jnp.float32
    )
    total_term = total_term + jnp.einsum(
        "ln,dn->ld", kv_grad_all[:, :kv_width], w_key, preferred_element_type=jnp.float32
    )
    total_term = total_term + jnp.einsum(
        "ln,dn->ld", kv_grad_all[:, kv_width:], w_value, preferred_element_type=jnp.float32
    )
    emb_inv_all = emb_all_f * inv_all[:, None]
    gain_terms = jnp.sum(total_term * emb_inv_all, axis=0)
    dot_terms = jnp.sum(total_term * (emb_all_f * norm_gain[None, :]), axis=1)
    col_terms = lax.psum(jnp.concatenate([gain_terms, dot_terms]), "col")
    grad_gain = col_terms[:feat]
    own_dots = lax.dynamic_slice(col_terms[feat:], (col_index * own_len,), (own_len,))
    total_dot = lax.psum(lax.psum(own_dots, "seq"), "row")
    col_sum = lax.psum_scatter(
        jnp.concatenate([branch_part, total_term], axis=1).astype(jnp.bfloat16),
        "col",
        scatter_dimension=0,
        tiled=True,
    ).astype(jnp.float32)
    branch_sum = col_sum[:, :feat]
    grad_normed = col_sum[:, feat:]
    layer_out = (residual + branch_sum).astype(jnp.bfloat16)

    inverse = lax.dynamic_slice(inv_all, (col_index * own_len,), (own_len,))
    scaled_grad = grad_normed * norm_gain[None, :]
    grad_input = (
        out_grad.astype(jnp.float32)
        + inverse[:, None] * scaled_grad
        - residual * (inverse**3 * total_dot / D)[:, None]
    ).astype(jnp.bfloat16)
    return (layer_out, grad_input, grad_gain, grad_wq, grad_wk, grad_wv, grad_wo)


def solution(mesh):
    placed = (
        P("col"),
        P("col"),
        P(),
        P(None, ("row", "seq")),
        P(None, ("row", "seq")),
        P(("row", "seq")),
        P(("row", "seq"), "col"),
        P(("row", "seq"), "col"),
        P(("row", "seq"), "col"),
        P("col", ("row", "seq")),
        P("col", ("row", "seq")),
    )
    return jax.shard_map(
        per_device,
        mesh=mesh,
        in_specs=placed,
        out_specs=(
            P("col", ("row", "seq")),
            P("col", ("row", "seq")),
            P(("row", "seq")),
            P(("row", "seq"), "col"),
            P(("row", "seq"), "col"),
            P(("row", "seq"), "col"),
            P("col", ("row", "seq")),
        ),
        check_vma=False,
    )
```

```python
import jax
import jax.numpy as jnp
from jax import lax
from jax.sharding import PartitionSpec as P
from jax.experimental import pallas as pl
from jax.experimental.pallas import tpu as pltpu

D = 8192
H = 64
KV = 8
HD = 128


epsilon = 1e-05
softcap = 20.0
rope_base = 500000.0
MAX_DOC = 768


def rotary_tables(positions, head_size):
    half_size = head_size // 2
    frequency = rope_base ** (-(jnp.arange(half_size, dtype=jnp.float32) * 2.0) / head_size)
    angles = positions.astype(jnp.float32)[:, None] * frequency[None, :]
    return (jnp.cos(angles), jnp.sin(angles))


def rotate_pairs(values, cosines, sines):
    half_size = values.shape[-1] // 2
    first_half = values[..., :half_size]
    second_half = values[..., half_size:]
    cos_part = cosines[:, None, :]
    sin_part = sines[:, None, :]
    return jnp.concatenate(
        [
            first_half * cos_part - second_half * sin_part,
            second_half * cos_part + first_half * sin_part,
        ],
        axis=-1,
    )


def rotate_back(values, cosines, sines):
    half_size = values.shape[-1] // 2
    first_half = values[..., :half_size]
    second_half = values[..., half_size:]
    cos_part = cosines[:, None, :]
    sin_part = sines[:, None, :]
    return jnp.concatenate(
        [
            first_half * cos_part + second_half * sin_part,
            second_half * cos_part - first_half * sin_part,
        ],
        axis=-1,
    )


def rope_round(values, positions):
    cosines, sines = rotary_tables(positions, HD)
    row_total = values.shape[0]
    return (
        rotate_pairs(values.reshape(row_total, -1, HD), cosines, sines)
        .reshape(row_total, -1)
        .astype(jnp.bfloat16)
    )


def to_blocks(values, n_row, n_seq):
    length, width = values.shape
    return values.reshape(n_row, length // n_row, n_seq, width // n_seq).transpose(0, 2, 1, 3)


def from_blocks(blocks):
    n_row, n_seq, rows, w = blocks.shape
    return blocks.transpose(0, 2, 1, 3).reshape(n_row * rows, n_seq * w)


def project_kernel(lhs_ref, wq_ref, wkv_ref, wo_ref, out_ref):
    feat = wq_ref.shape[0]
    qw = wq_ref.shape[1]
    kw = wkv_ref.shape[1]
    ow = wo_ref.shape[0]
    emb = lhs_ref[:, :feat]
    og = lhs_ref[:, feat:]
    out_ref[:, :qw] = jnp.dot(emb, wq_ref[...], preferred_element_type=jnp.float32)
    out_ref[:, qw : qw + kw] = jnp.dot(emb, wkv_ref[...], preferred_element_type=jnp.float32)
    out_ref[:, qw + kw :] = lax.dot_general(
        og, wo_ref[...], (((1,), (1,)), ((), ())), preferred_element_type=jnp.float32
    )


def project_blocks(lhs, wq, wkv, wo, n_row, n_seq, out_w):
    length, lw = lhs.shape
    feat = wq.shape[0]
    qw = wq.shape[1] // n_seq
    kw = HD
    ow = wo.shape[0] // n_seq
    rows = length // n_row
    flops = 2 * length * feat * (n_seq * (qw + kw + ow))
    return pl.pallas_call(
        project_kernel,
        grid=(n_seq, n_row),
        in_specs=[
            pl.BlockSpec((rows, lw), lambda s, r: (r, 0)),
            pl.BlockSpec((feat, qw), lambda s, r: (0, s)),
            pl.BlockSpec((feat, kw), lambda s, r: (0, s % 2)),
            pl.BlockSpec((ow, feat), lambda s, r: (s, 0)),
        ],
        out_specs=pl.BlockSpec((rows, out_w), lambda s, r: (r * n_seq + s, 0)),
        out_shape=jax.ShapeDtypeStruct((n_row * n_seq * rows, out_w), jnp.float32),
        cost_estimate=pl.CostEstimate(
            flops=flops,
            transcendentals=0,
            bytes_accessed=lhs.size * 2 + (wq.size + wkv.size + wo.size) * 2
            + n_row * n_seq * rows * out_w * 4,
        ),
    )(lhs, wq, wkv, wo)


def attention_kernel(
    q_ref, do_ref, k_ref, v_ref, qpos_ref, qseg_ref, kpos_ref, kseg_ref,
    out_ref, gq_ref, gk_ref, gv_ref,
):
    head = pl.program_id(0)
    score_scale = HD ** (-0.5)
    query = q_ref[0]
    dout = do_ref[0]
    key = k_ref[...]
    value = v_ref[...]
    allowed = (kpos_ref[...] <= qpos_ref[...]) & (kseg_ref[...] == qseg_ref[...])
    nt = (((1,), (1,)), ((), ()))
    tn = (((0,), (0,)), ((), ()))
    raw_scores = (
        lax.dot_general(query, key, nt, preferred_element_type=jnp.float32) * score_scale
    )
    capped = softcap * jnp.tanh(raw_scores / softcap)
    weights = jnp.where(allowed, jnp.exp(capped), 0.0)
    totals = jnp.sum(weights, axis=1, keepdims=True)
    attended = jnp.dot(
        weights.astype(jnp.bfloat16), value, preferred_element_type=jnp.float32
    )
    out_ref[0] = (attended / totals).astype(out_ref.dtype)
    probs = weights / totals
    prob_grads = lax.dot_general(dout, value, nt, preferred_element_type=jnp.float32)
    row_dots = jnp.sum(probs * prob_grads, axis=1, keepdims=True)
    grad_scores = (
        probs * (prob_grads - row_dots) * (1.0 - (capped / softcap) ** 2) * score_scale
    ).astype(jnp.bfloat16)
    gq_ref[0] = jnp.dot(grad_scores, key, preferred_element_type=jnp.float32)
    gk_term = lax.dot_general(grad_scores, query, tn, preferred_element_type=jnp.float32)
    gv_term = lax.dot_general(
        probs.astype(jnp.bfloat16), dout, tn, preferred_element_type=jnp.float32
    )

    @pl.when(head == 0)
    def _():
        gk_ref[...] = gk_term
        gv_ref[...] = gv_term

    @pl.when(head != 0)
    def _():
        gk_ref[...] += gk_term
        gv_ref[...] += gv_term


def attention_block(q, dout, key, value, qpos, qseg, kpos, kseg):
    heads, rows, hd = q.shape
    win = key.shape[0]
    full = lambda h: (0, 0)
    per_head = lambda h: (h, 0, 0)
    return pl.pallas_call(
        attention_kernel,
        grid=(heads,),
        in_specs=[
            pl.BlockSpec((1, rows, hd), per_head),
            pl.BlockSpec((1, rows, hd), per_head),
            pl.BlockSpec((win, hd), full),
            pl.BlockSpec((win, hd), full),
            pl.BlockSpec((rows, 1), full),
            pl.BlockSpec((rows, 1), full),
            pl.BlockSpec((1, win), full),
            pl.BlockSpec((1, win), full),
        ],
        out_specs=[
            pl.BlockSpec((1, rows, hd), per_head),
            pl.BlockSpec((1, rows, hd), per_head),
            pl.BlockSpec((win, hd), full),
            pl.BlockSpec((win, hd), full),
        ],
        out_shape=[
            jax.ShapeDtypeStruct((heads, rows, hd), jnp.bfloat16),
            jax.ShapeDtypeStruct((heads, rows, hd), jnp.float32),
            jax.ShapeDtypeStruct((win, hd), jnp.float32),
            jax.ShapeDtypeStruct((win, hd), jnp.float32),
        ],
        compiler_params=pltpu.CompilerParams(
            dimension_semantics=("arbitrary",), vmem_limit_bytes=48 * 1024 * 1024
        ),
        cost_estimate=pl.CostEstimate(
            flops=12 * heads * rows * win * hd,
            transcendentals=2 * heads * rows * win,
            bytes_accessed=4 * heads * rows * hd * 2 + 4 * win * hd * 4,
        ),
    )(q, dout, key, value, qpos, qseg, kpos, kseg)


def per_device(
    motion_ids,
    audio_ids,
    segment_ids,
    motion_table,
    audio_table,
    norm_gain,
    w_query,
    w_key,
    w_value,
    w_out,
    out_grad,
):
    seq_len = segment_ids.shape[0]
    n_row = lax.axis_size("row")
    n_seq = lax.axis_size("seq")
    n_col = lax.axis_size("col")
    row_index = lax.axis_index("row")
    seq_index = lax.axis_index("seq")
    col_index = lax.axis_index("col")
    n_rs = n_row * n_seq
    block_len = seq_len // n_rs
    quarter_len = seq_len // n_row
    own_len = seq_len // n_col
    feat = motion_table.shape[1]
    query_width = w_query.shape[1]
    kv_width = w_key.shape[1]
    head_count = query_width // HD // n_seq
    part_w = head_count * HD
    score_scale = HD ** (-0.5)
    assert kv_width == HD and part_w == 2 * HD

    embedded = (
        jnp.take(motion_table, motion_ids, axis=0).astype(jnp.float32)
        + jnp.take(audio_table, audio_ids, axis=0).astype(jnp.float32)
    ).astype(jnp.bfloat16)
    residual = embedded.astype(jnp.float32)

    both_all = lax.all_gather(
        jnp.concatenate([embedded, out_grad], axis=1), "col", axis=0, tiled=True
    )
    emb_all = both_all[:, :feat]
    grad_all = both_all[:, feat:]
    emb_all_f = emb_all.astype(jnp.float32)
    gain_col = norm_gain[:, None]
    wq_gain = (w_query.astype(jnp.float32) * gain_col).astype(jnp.bfloat16)
    wkv_gain = (
        jnp.concatenate([w_key, w_value], axis=1).astype(jnp.float32) * gain_col
    ).astype(jnp.bfloat16)
    out_w = part_w + HD + part_w
    squares = lax.psum(lax.psum(jnp.sum(emb_all_f * emb_all_f, axis=1), "seq"), "row")
    inv_all = lax.rsqrt(squares / D + epsilon)
    blocks = project_blocks(both_all, wq_gain, wkv_gain, w_out, n_row, n_seq, out_w)
    got = lax.psum_scatter(blocks, ("row", "seq"), scatter_dimension=0, tiled=True)

    q_raw = got[:, :part_w]
    kv_raw = got[:, part_w : part_w + HD]
    d_raw = got[:, part_w + HD : 2 * part_w + HD]
    inv_q = lax.dynamic_slice(inv_all, (row_index * quarter_len,), (quarter_len,))

    query_pos = row_index * quarter_len + jnp.arange(quarter_len, dtype=jnp.int32)
    queries = rope_round(q_raw * inv_q[:, None], query_pos)
    kv_scaled = kv_raw * inv_q[:, None]
    kv_piece = jnp.where(
        seq_index % 2 == 0, rope_round(kv_scaled, query_pos), kv_scaled.astype(jnp.bfloat16)
    )
    out_heads = d_raw.astype(jnp.bfloat16).reshape(quarter_len, head_count, HD)

    half_len = quarter_len // 2
    kv_half = lax.dynamic_slice(kv_piece, ((seq_index // 2) * half_len, 0), (half_len, HD))
    kv_gath = lax.all_gather(kv_half, ("row", "seq"), axis=0, tiled=True).reshape(
        n_row, 2, 2, half_len, HD
    )
    key_all = kv_gath[:, :, 0].reshape(seq_len, HD)
    value_all = kv_gath[:, :, 1].reshape(seq_len, HD)

    doc_back = -(-(MAX_DOC - 1) // quarter_len) * quarter_len
    win = min(seq_len, quarter_len + doc_back)
    win_start = jnp.clip(row_index * quarter_len - doc_back, 0, seq_len - win)
    key_pos = win_start + jnp.arange(win, dtype=jnp.int32)
    key_sel = lax.dynamic_slice(key_all, (win_start, 0), (win, HD))
    value_sel = lax.dynamic_slice(value_all, (win_start, 0), (win, HD))
    key_seg = lax.dynamic_slice(segment_ids, (win_start,), (win,))
    query_seg = jnp.take(segment_ids, query_pos)
    attn_heads, grad_query_heads, grad_key_part, grad_value_part = attention_block(
        queries.reshape(quarter_len, head_count, HD).transpose(1, 0, 2),
        out_heads.transpose(1, 0, 2),
        key_sel,
        value_sel,
        query_pos[:, None],
        query_seg[:, None],
        key_pos[None, :],
        key_seg[None, :],
    )
    attn_out = attn_heads.transpose(1, 0, 2).reshape(quarter_len, part_w)
    grad_query = grad_query_heads.transpose(1, 0, 2)
    cos_all, sin_all = rotary_tables(key_pos, HD)
    grad_key_rot = rotate_back(grad_key_part[:, None, :], cos_all, sin_all).reshape(
        win, kv_width
    )
    kv_grad_win = jnp.concatenate([grad_key_rot, grad_value_part], axis=1).astype(jnp.bfloat16)
    cos_query, sin_query = rotary_tables(query_pos, HD)
    grad_query_round = (
        rotate_back(grad_query, cos_query, sin_query)
        .reshape(quarter_len, part_w)
        .astype(jnp.bfloat16)
    )
    back_rows = 2 * quarter_len + win + 8
    back_all = lax.all_gather(
        jnp.concatenate(
            [attn_out, grad_query_round, kv_grad_win, jnp.zeros((8, part_w), jnp.bfloat16)], axis=0
        ),
        ("row", "seq"),
        axis=0,
        tiled=True,
    ).reshape(n_rs, back_rows, part_w)
    out_all = from_blocks(back_all[:, :quarter_len].reshape(n_row, n_seq, quarter_len, part_w))
    grad_query_all = from_blocks(
        back_all[:, quarter_len : 2 * quarter_len].reshape(n_row, n_seq, quarter_len, part_w)
    )
    kv_terms = (
        back_all[:, 2 * quarter_len : 2 * quarter_len + win]
        .astype(jnp.float32)
        .reshape(n_row, n_seq, win, part_w)
        .sum(axis=1)
    )
    kv_grad_f = jnp.zeros((seq_len, part_w), jnp.float32)
    for quarter in range(n_row):
        first = min(max(quarter * quarter_len - doc_back, 0), seq_len - win)
        kv_grad_f = kv_grad_f.at[first : first + win].add(kv_terms[quarter])
    kv_grad_all = kv_grad_f.astype(jnp.bfloat16)

    normed_all = (emb_all_f * inv_all[:, None] * norm_gain[None, :]).astype(jnp.bfloat16)
    grad_wo = jnp.einsum("ln,ld->nd", out_all, grad_all, preferred_element_type=jnp.float32)
    grad_wq = jnp.einsum(
        "ld,ln->dn", normed_all, grad_query_all, preferred_element_type=jnp.float32
    )
    grad_wk = jnp.einsum(
        "ld,ln->dn", normed_all, kv_grad_all[:, :kv_width], preferred_element_type=jnp.float32
    )
    grad_wv = jnp.einsum(
        "ld,ln->dn", normed_all, kv_grad_all[:, kv_width:], preferred_element_type=jnp.float32
    )

    branch_part = jnp.dot(out_all, w_out, preferred_element_type=jnp.float32)
    total_term = jnp.einsum(
        "ln,dn->ld", grad_query_all, w_query, preferred_element_type=jnp.float32
    )
    total_term = total_term + jnp.einsum(
        "ln,dn->ld", kv_grad_all[:, :kv_width], w_key, preferred_element_type=jnp.float32
    )
    total_term = total_term + jnp.einsum(
        "ln,dn->ld", kv_grad_all[:, kv_width:], w_value, preferred_element_type=jnp.float32
    )
    emb_inv_all = emb_all_f * inv_all[:, None]
    gain_terms = jnp.sum(total_term * emb_inv_all, axis=0)
    dot_terms = jnp.sum(total_term * (emb_all_f * norm_gain[None, :]), axis=1)
    col_terms = lax.psum(jnp.concatenate([gain_terms, dot_terms]), "col")
    grad_gain = col_terms[:feat]
    own_dots = lax.dynamic_slice(col_terms[feat:], (col_index * own_len,), (own_len,))
    total_dot = lax.psum(lax.psum(own_dots, "seq"), "row")
    col_sum = lax.psum_scatter(
        jnp.concatenate([branch_part, total_term], axis=1).astype(jnp.bfloat16),
        "col",
        scatter_dimension=0,
        tiled=True,
    ).astype(jnp.float32)
    branch_sum = col_sum[:, :feat]
    grad_normed = col_sum[:, feat:]
    layer_out = (residual + branch_sum).astype(jnp.bfloat16)

    inverse = lax.dynamic_slice(inv_all, (col_index * own_len,), (own_len,))
    scaled_grad = grad_normed * norm_gain[None, :]
    grad_input = (
        out_grad.astype(jnp.float32)
        + inverse[:, None] * scaled_grad
        - residual * (inverse**3 * total_dot / D)[:, None]
    ).astype(jnp.bfloat16)
    return (layer_out, grad_input, grad_gain, grad_wq, grad_wk, grad_wv, grad_wo)


def solution(mesh):
    placed = (
        P("col"),
        P("col"),
        P(),
        P(None, ("row", "seq")),
        P(None, ("row", "seq")),
        P(("row", "seq")),
        P(("row", "seq"), "col"),
        P(("row", "seq"), "col"),
        P(("row", "seq"), "col"),
        P("col", ("row", "seq")),
        P("col", ("row", "seq")),
    )
    return jax.shard_map(
        per_device,
        mesh=mesh,
        in_specs=placed,
        out_specs=(
            P("col", ("row", "seq")),
            P("col", ("row", "seq")),
            P(("row", "seq")),
            P(("row", "seq"), "col"),
            P(("row", "seq"), "col"),
            P(("row", "seq"), "col"),
            P("col", ("row", "seq")),
        ),
        check_vma=False,
    )
```
